256 devices in a mesh: ty: 16 (over y, z_hi), tx: 16 (over x, z_lo, core).
Axes of the slice: x: 4, y: 4, z: 8 (z_hi: 4, z_lo: 2; z = z_hi * 2 + z_lo), core: 2. Of those that a mesh axis runs over, the one named last changes fastest.
Arguments:
- object_tiles: float32 [2, 2, 4096, 4096], P(None, None, 'ty', 'tx'), may hold values from -5 to 5
- probe_field: float32 [2, 256, 256], replicated, may hold values from -6 to 6
- prop_angle: float32 [256, 256], replicated, may hold values from -3.140625 to 3.140625
- scan_offsets: int32 [2, 16, 16, 2, 2], P(None, 'ty', 'tx'), may hold values from 0 to 255, as said below
- probe_counts: int32 [2, 16, 16], P(None, 'ty', 'tx'), may hold values from 0 to 2, as said below
- amplitudes: float32 [2, 16, 16, 2, 256, 256], P(None, 'ty', 'tx'), may hold values from 0 to 2.5
Outputs:
- object_out: float32 [2, 2, 4096, 4096], P(None, None, 'ty', 'tx')
The draws below stay inside these ranges and needn't reach their ends.
Inputs may be any that keep to these rules, and one draw needn't show every extreme that they name: `probe_counts`: every tile has at most 2 live slots in an iteration, and some tile has exactly 2 in every iteration; slots at or past a tile's count are not used. `scan_offsets`: on tiles of the last tile row the row offset is at most 0, and on tiles of the last tile column the column offset is at most 0, so every window lies inside the object.
All inputs are finite; a program needn't handle non-finite values.
Results may differ from the reference program's by a relative error of at most 0.0003.
Values sent between devices are 32-bit elements; how exact they have to be, the bound alone decides.
No kernel may reach another device: no remote copies, remote signals or barrier semaphores. Data moves between devices by JAX's collectives and lax.ppermute only.
A program may use at most 128 MiB of HBM per device.

```python
import jax
import jax.numpy as jnp
from jax import lax

PROBE = 256
TILE = 256
P_MAX = 2
ITERS = 2
TILE_ROWS = 16
TILE_COLS = 16
NY = 4096
NX = 4096


def draw_scan_offsets(key, part):
    array_shape = (ITERS, TILE_ROWS, TILE_COLS, P_MAX, 2)
    raw_bits = jax.random.randint(key, array_shape, 0, 1 << 20)
    iter_ids = lax.broadcasted_iota(jnp.int32, array_shape, 0)
    row_ids = lax.broadcasted_iota(jnp.int32, array_shape, 1)
    col_ids = lax.broadcasted_iota(jnp.int32, array_shape, 2)
    slot_ids = lax.broadcasted_iota(jnp.int32, array_shape, 3)
    coord_ids = lax.broadcasted_iota(jnp.int32, array_shape, 4)
    last_edge = jnp.where(coord_ids == 0, row_ids == TILE_ROWS - 1, col_ids == TILE_COLS - 1)
    upper_bound = jnp.where(last_edge, TILE - PROBE + 1, TILE)
    values = raw_bits % upper_bound
    picked_idx = jax.random.randint(jax.random.fold_in(key, 7), (4,), 0, 1 << 20)
    far_row = picked_idx[0] % (TILE_ROWS - 1)
    far_col = picked_idx[1] % (TILE_COLS - 1)
    near_row = picked_idx[2] % TILE_ROWS
    near_col = picked_idx[3] % TILE_COLS
    far_spot = (iter_ids == 0) & (row_ids == far_row) & (col_ids == far_col) & (slot_ids == 0)
    values = jnp.where(far_spot, TILE - 1, values)
    near_spot = (iter_ids == 0) & (row_ids == near_row) & (col_ids == near_col) & (slot_ids == P_MAX - 1)
    values = jnp.where(near_spot, 0, values)
    return values.astype(jnp.int32)


def draw_probe_counts(key, part):
    array_shape = (ITERS, TILE_ROWS, TILE_COLS)
    base_counts = jax.random.randint(key, array_shape, 0, P_MAX + 1)
    busiest = jax.random.randint(jax.random.fold_in(key, 11), (ITERS, 1, 1), 0, TILE_ROWS * TILE_COLS)
    flat_ids = lax.broadcasted_iota(jnp.int32, array_shape, 1) * TILE_COLS + lax.broadcasted_iota(jnp.int32, array_shape, 2)
    return jnp.where(flat_ids == busiest, P_MAX, base_counts).astype(jnp.int32)


def steps_of(stream_key, extent, split, smallest, largest):
    level = 1.0
    for dim, parts in split:
        heights = jax.random.uniform(jax.random.fold_in(jax.random.fold_in(stream_key, 6), dim), (parts,), jnp.float32, smallest / len(split), largest / len(split))
        level = level * jnp.repeat(jnp.exp(heights), extent[dim] // parts).reshape((-1,) + (1,) * (len(extent) - 1 - dim))
    return level


def normal_values(stream_key, extent, deviation, bound, shards=(), held_as=jnp.bfloat16):
    level = steps_of(stream_key, extent, shards, -0.22, 0.18) if shards else 1.0
    drawn = jax.random.normal(stream_key, extent, jnp.float32) * deviation * level
    return jnp.minimum(jnp.maximum(drawn, -bound), bound).astype(held_as)


def setup_inputs(seed: int = 0) -> dict:
    key_list = jax.random.split(jax.random.key(seed), 7)
    object_tiles = normal_values(key_list[0], (2, 2, NY, NX), 0.7, 5.0, ((2, 16), (3, 16)), jnp.float32)
    probe_field = normal_values(key_list[1], (2, PROBE, PROBE), 1.0, 6.0, (), jnp.float32)
    prop_angle = jnp.clip(jax.random.uniform(key_list[2], (PROBE, PROBE), jnp.float32, -3.140625, 3.140625), -3.140625, 3.140625)
    scan_offsets = draw_scan_offsets(jax.random.fold_in(key_list[6], 71), 0)
    probe_counts = draw_probe_counts(jax.random.fold_in(key_list[6], 71), 0)
    amplitudes = jnp.clip(2.5 * jax.random.uniform(key_list[5], (ITERS, TILE_ROWS, TILE_COLS, P_MAX, PROBE, PROBE), jnp.float32) ** steps_of(key_list[5], (ITERS, TILE_ROWS, TILE_COLS, P_MAX, PROBE, PROBE), ((1, 16), (2, 16)), -0.2, 0.2), 0.0, 2.5)
    return {"object_tiles": object_tiles, "probe_field": probe_field, "prop_angle": prop_angle, "scan_offsets": scan_offsets, "probe_counts": probe_counts, "amplitudes": amplitudes}


soft_floor = 0.01
step_size = 0.25

def spectrum(real_part, imag_part, inverse):
    field = lax.complex(real_part, imag_part)
    if inverse:
        result = jnp.fft.ifft2(field, norm='ortho')
    else:
        result = jnp.fft.fft2(field, norm='ortho')
    return (jnp.real(result), jnp.imag(result))

def window_gradient(window, probe_field, kernel_re, kernel_im, measured_amp, transform):
    one_re, one_im = (window[0, 0], window[0, 1])
    two_re, two_im = (window[1, 0], window[1, 1])
    probe_re, probe_im = (probe_field[0], probe_field[1])
    first_re = probe_re * one_re - probe_im * one_im
    first_im = probe_re * one_im + probe_im * one_re
    freq_re, freq_im = transform(first_re, first_im, False)
    moved_re = freq_re * kernel_re - freq_im * kernel_im
    moved_im = freq_re * kernel_im + freq_im * kernel_re
    mid_re, mid_im = transform(moved_re, moved_im, True)
    second_re = mid_re * two_re - mid_im * two_im
    second_im = mid_re * two_im + mid_im * two_re
    far_re, far_im = transform(second_re, second_im, False)
    magnitude = jnp.sqrt(far_re * far_re + far_im * far_im + soft_floor)
    factor = 1.0 - measured_amp / magnitude
    back_re, back_im = transform(far_re * factor, far_im * factor, True)
    grad_two_re = mid_re * back_re + mid_im * back_im
    grad_two_im = mid_re * back_im - mid_im * back_re
    carry_re = two_re * back_re + two_im * back_im
    carry_im = two_re * back_im - two_im * back_re
    spec_re, spec_im = transform(carry_re, carry_im, False)
    turned_re = spec_re * kernel_re + spec_im * kernel_im
    turned_im = spec_im * kernel_re - spec_re * kernel_im
    early_re, early_im = transform(turned_re, turned_im, True)
    grad_one_re = probe_re * early_re + probe_im * early_im
    grad_one_im = probe_re * early_im - probe_im * early_re
    return jnp.stack([jnp.stack([grad_one_re, grad_one_im]), jnp.stack([grad_two_re, grad_two_im])])

def reference(object_tiles, probe_field, prop_angle, scan_offsets, probe_counts, amplitudes):
    kernel_re = jnp.cos(prop_angle)
    kernel_im = jnp.sin(prop_angle)
    slot_total = TILE_ROWS * TILE_COLS * P_MAX
    slot_ids = lax.iota(jnp.int32, slot_total)
    tile_ids = slot_ids // P_MAX
    row_ids = tile_ids // TILE_COLS
    col_ids = tile_ids % TILE_COLS
    slot_in_tile = slot_ids % P_MAX
    zero_index = jnp.zeros((), jnp.int32)
    current = object_tiles
    for iteration in range(ITERS):
        offsets = scan_offsets[iteration].reshape(slot_total, 2)
        counts_here = probe_counts[iteration].reshape(TILE_ROWS * TILE_COLS)
        live_mask = (slot_in_tile < counts_here[tile_ids]).astype(jnp.float32)
        corner_rows = (row_ids * TILE + offsets[:, 0]).astype(jnp.int32)
        corner_cols = (col_ids * TILE + offsets[:, 1]).astype(jnp.int32)
        measured = amplitudes[iteration].reshape(slot_total, PROBE, PROBE)

        def accumulate(running, inputs, frozen=current):
            corner_row, corner_col, weight, measured_amp = inputs
            start_index = (zero_index, zero_index, corner_row.astype(jnp.int32), corner_col.astype(jnp.int32))
            window = lax.dynamic_slice(frozen, start_index, (2, 2, PROBE, PROBE))
            contrib = window_gradient(window, probe_field, kernel_re, kernel_im, measured_amp, spectrum) * weight
            placed = lax.dynamic_slice(running, start_index, (2, 2, PROBE, PROBE)) + contrib
            return (lax.dynamic_update_slice(running, placed, start_index), None)
        gradient, unused = lax.scan(accumulate, jnp.zeros_like(current), (corner_rows, corner_cols, live_mask, measured))
        current = current - step_size * gradient
    return current
```

```python
import numpy as np

import jax
import jax.numpy as jnp
from jax import lax
from jax.experimental import pallas as pl
from jax.experimental.pallas import tpu as pltpu
from jax.sharding import PartitionSpec as P

ITERS = 2
SLOTS = 2
SIDE = 256
HALF = SIDE // 2

soft_floor = 0.01
step_size = 0.25


def dft_tables():
    k = np.arange(HALF)
    stack = []
    for parity in (0, 1):
        angle = 2.0 * np.pi * ((2 * k[:, None] + parity) * k[None, :] % SIDE) / SIDE
        cos, sin = np.cos(angle) / 16.0, np.sin(angle) / 16.0
        stack.append(np.block([[cos, sin], [-sin, cos]]))
    both = np.stack([np.stack(stack), np.stack([t.T for t in stack])])
    high = both.astype(jnp.bfloat16)
    low = (both - high.astype(np.float64)).astype(jnp.bfloat16)
    return np.stack([high, low], axis=2)


def shifted(value, axis, steps):
    count = lax.axis_size(axis)
    first, last = (max(0, -steps), min(count, count - steps))
    return lax.ppermute(value, axis, [(source, source + steps) for source in range(first, last)])


def split(value):
    high = value.astype(jnp.bfloat16)
    return high, (value - high.astype(jnp.float32)).astype(jnp.bfloat16)


def dot(left, right):
    return jnp.dot(left, right, preferred_element_type=jnp.float32)


def table_left(tables, flip, parity, value):
    high, low = split(value)
    t_high, t_low = tables[flip, parity, 0], tables[flip, parity, 1]
    return dot(t_high, high) + (dot(t_high, low) + dot(t_low, high))


def table_right(tables, flip, parity, value):
    high, low = split(value)
    t_high, t_low = tables[flip, parity, 0], tables[flip, parity, 1]
    return dot(high, t_high) + (dot(low, t_high) + dot(high, t_low))


def rows_cat(a, b):
    return jnp.concatenate([a, b], axis=0)


def lanes_cat(a, b):
    return jnp.concatenate([a, b], axis=1)


def forward(tables, re, im):
    ra, rb, ia, ib = re[:HALF], re[HALF:], im[:HALF], im[HALF:]
    even = table_left(tables, 0, 0, rows_cat(ra + rb, ia + ib))
    odd = table_left(tables, 0, 1, rows_cat(ra - rb, ia - ib))
    real = rows_cat(even[:HALF], odd[:HALF])
    imag = rows_cat(even[HALF:], odd[HALF:])
    ra, rb, ia, ib = real[:, :HALF], real[:, HALF:], imag[:, :HALF], imag[:, HALF:]
    return (
        table_right(tables, 1, 0, lanes_cat(ra + rb, ia + ib)),
        table_right(tables, 1, 1, lanes_cat(ra - rb, ia - ib)),
    )


def inverse(tables, even, odd):
    even = table_right(tables, 0, 0, even)
    odd = table_right(tables, 0, 1, odd)
    real = lanes_cat(even[:, :HALF] + odd[:, :HALF], even[:, :HALF] - odd[:, :HALF])
    imag = lanes_cat(even[:, HALF:] + odd[:, HALF:], even[:, HALF:] - odd[:, HALF:])
    even = table_left(tables, 1, 0, rows_cat(real[:HALF], imag[:HALF]))
    odd = table_left(tables, 1, 1, rows_cat(real[HALF:], imag[HALF:]))
    return (
        rows_cat(even[:HALF] + odd[:HALF], even[:HALF] - odd[:HALF]),
        rows_cat(even[HALF:] + odd[HALF:], even[HALF:] - odd[HALF:]),
    )


def masks(off_ref, iteration, slot):
    row = off_ref[iteration, slot, 0]
    col = off_ref[iteration, slot, 1]
    below = lax.broadcasted_iota(jnp.int32, (SIDE, SIDE), 0) < row
    right = lax.broadcasted_iota(jnp.int32, (SIDE, SIDE), 1) < col
    return below, right


def picked(below, right, own, rgt, low, dia, plane):
    upper = jnp.where(right, rgt[plane], own[plane])
    lower = jnp.where(right, dia[plane], low[plane])
    return jnp.where(below, lower, upper)


def placed(below, right, value, plane, stay, move):
    zero = jnp.zeros_like(value)
    left_part = jnp.where(right, zero, value)
    right_part = jnp.where(right, value, zero)
    stay[0, plane] += jnp.where(below, zero, left_part)
    stay[1, plane] += jnp.where(below, left_part, zero)
    move[0, plane] += jnp.where(below, zero, right_part)
    move[1, plane] += jnp.where(below, right_part, zero)


def prepare_kernel(off_ref, probe_ref, cos_ref, sin_ref, amp_ref, perm_ref,
                   rolled_ref, prop_ref, ampl_ref, twice):
    def reorder(src):
        rest = src[...]
        total = None
        for _ in range(3):
            part = rest.astype(jnp.bfloat16)
            rest = rest - part.astype(jnp.float32)
            part = dot(dot(perm_ref[0], part).astype(jnp.bfloat16), perm_ref[1])
            total = part if total is None else total + part
        return total

    def put(dst, value):
        dst[0] = value[:, :HALF]
        dst[1] = value[:, HALF:]

    def tile_loop(index, carry):
        it, slot = index // SLOTS, index % SLOTS
        row = off_ref[it, slot, 0]
        col = off_ref[it, slot, 1]
        for plane in range(2):
            start = pl.multiple_of(SIDE - 8 - row // 8 * 8, 8)
            turned = pltpu.roll(twice[plane, pl.ds(start, SIDE + 8), :], row % 8, 0)
            rolled_ref[it, slot, plane] = pltpu.roll(turned[8:], col, 1)
        put(ampl_ref.at[it, slot], reorder(amp_ref.at[it, slot]))
        return carry

    for plane in range(2):
        twice[plane, :SIDE] = probe_ref[plane]
        twice[plane, SIDE:] = probe_ref[plane]
    put(prop_ref.at[0], reorder(cos_ref))
    put(prop_ref.at[1], reorder(sin_ref))
    lax.fori_loop(0, ITERS * SLOTS, tile_loop, 0)


def first_kernel(iteration, off_ref, cnt_ref, own, rgt, low, dia, rolled, prop, tables, mid_ref):
    def body(slot, carry):
        below, right = masks(off_ref, iteration, slot)
        one_re = picked(below, right, own, rgt, low, dia, 0)
        one_im = picked(below, right, own, rgt, low, dia, 1)
        p_re, p_im = rolled[iteration, slot, 0], rolled[iteration, slot, 1]
        spec = forward(tables, p_re * one_re - p_im * one_im, p_re * one_im + p_im * one_re)
        moved = []
        for q in range(2):
            re, im = spec[q][:, :HALF], spec[q][:, HALF:]
            h_re, h_im = prop[0, q], prop[1, q]
            moved.append(lanes_cat(re * h_re - im * h_im, re * h_im + im * h_re))
        mid_ref[slot, 0], mid_ref[slot, 1] = inverse(tables, *moved)
        return carry

    lax.fori_loop(0, cnt_ref[iteration], body, 0)


def second_kernel(iteration, off_ref, cnt_ref, own, rgt, low, dia, mid_ref, ampl, tables,
                  stay, move, carry_ref):
    stay[...] = jnp.zeros_like(stay)
    move[...] = jnp.zeros_like(move)

    def body(slot, carry):
        below, right = masks(off_ref, iteration, slot)
        two_re = picked(below, right, own, rgt, low, dia, 0)
        two_im = picked(below, right, own, rgt, low, dia, 1)
        m_re, m_im = mid_ref[slot, 0], mid_ref[slot, 1]
        far = forward(tables, m_re * two_re - m_im * two_im, m_re * two_im + m_im * two_re)
        chi = []
        for q in range(2):
            re, im = far[q][:, :HALF], far[q][:, HALF:]
            factor = 1.0 - ampl[iteration, slot, q] * lax.rsqrt(re * re + im * im + soft_floor)
            chi.append(lanes_cat(re * factor, im * factor))
        b_re, b_im = inverse(tables, *chi)
        placed(below, right, m_re * b_re + m_im * b_im, 0, stay, move)
        placed(below, right, m_re * b_im - m_im * b_re, 1, stay, move)
        carry_ref[slot, 0] = two_re * b_re + two_im * b_im
        carry_ref[slot, 1] = two_re * b_im - two_im * b_re
        return carry

    lax.fori_loop(0, cnt_ref[iteration], body, 0)


def third_kernel(iteration, off_ref, cnt_ref, carry_ref, rolled, prop, tables, stay, move):
    stay[...] = jnp.zeros_like(stay)
    move[...] = jnp.zeros_like(move)

    def body(slot, carry):
        below, right = masks(off_ref, iteration, slot)
        spec = forward(tables, carry_ref[slot, 0], carry_ref[slot, 1])
        turned = []
        for q in range(2):
            re, im = spec[q][:, :HALF], spec[q][:, HALF:]
            h_re, h_im = prop[0, q], prop[1, q]
            turned.append(lanes_cat(re * h_re + im * h_im, im * h_re - re * h_im))
        e_re, e_im = inverse(tables, *turned)
        p_re, p_im = rolled[iteration, slot, 0], rolled[iteration, slot, 1]
        placed(below, right, p_re * e_re + p_im * e_im, 0, stay, move)
        placed(below, right, p_re * e_im - p_im * e_re, 1, stay, move)
        return carry

    lax.fori_loop(0, cnt_ref[iteration], body, 0)


SMEM = pl.BlockSpec(memory_space=pltpu.SMEM)
VMEM = pl.BlockSpec(memory_space=pltpu.VMEM)
LIMIT = 24 * 1024 * 1024


def f32(*shape):
    return jax.ShapeDtypeStruct(shape, jnp.float32)


def call(body, name, scalars, arrays, outs, scratch=()):
    args = [*scalars, *arrays]
    return pl.pallas_call(
        body,
        name=name,
        out_shape=outs,
        in_specs=[SMEM] * len(scalars) + [VMEM] * len(arrays),
        out_specs=[VMEM] * len(outs),
        scratch_shapes=scratch,
        compiler_params=pltpu.CompilerParams(vmem_limit_bytes=LIMIT),
        cost_estimate=pl.CostEstimate(flops=4 * 10**9, bytes_accessed=8 * 2**20, transcendentals=0),
    )(*args)


def shards(object_tiles, probe_field, prop_angle, scan_offsets, probe_counts, amplitudes):
    tables = jnp.asarray(dft_tables())
    lane = np.arange(SIDE)
    source = np.concatenate([lane[0::2], lane[1::2]])
    perm = np.zeros((SIDE, SIDE), np.float32)
    perm[source, lane] = 1.0
    perm = jnp.asarray(np.stack([perm.T, perm]).astype(jnp.bfloat16))
    offsets = scan_offsets.reshape(ITERS, SLOTS, 2)
    counts = probe_counts.reshape(ITERS)
    measured = amplitudes.reshape(ITERS, SLOTS, SIDE, SIDE)

    own = [object_tiles[0], object_tiles[1]]
    low = [shifted(own[0], "ty", -1), shifted(own[1], "ty", -1)]
    rgt = [shifted(own[0], "tx", -1), shifted(own[1], "tx", -1)]
    dia = [shifted(low[0], "tx", -1), shifted(low[1], "tx", -1)]

    rolled, prop, ampl = call(
        prepare_kernel, "prepare", [offsets],
        [probe_field, jnp.cos(prop_angle), jnp.sin(prop_angle), measured, perm],
        [f32(ITERS, SLOTS, 2, SIDE, SIDE), f32(2, 2, SIDE, HALF), f32(ITERS, SLOTS, 2, SIDE, HALF)],
        [pltpu.VMEM((2, 2 * SIDE, SIDE), jnp.float32)],
    )
    pair = f32(2, 2, SIDE, SIDE)

    for iteration in range(ITERS):
        def bind(kernel, iteration=iteration):
            return lambda *refs: kernel(iteration, *refs)

        scalars = [offsets, counts]
        (mid,) = call(bind(first_kernel), "first", scalars,
                      [own[0], rgt[0], low[0], dia[0], rolled, prop, tables], [pair])
        stay2, move2, carry = call(bind(second_kernel), "second", scalars,
                                   [own[1], rgt[1], low[1], dia[1], mid, ampl, tables], [pair] * 3)
        stay1, move1 = call(bind(third_kernel), "third", scalars,
                            [carry, rolled, prop, tables], [pair] * 2)
        stay, move = [stay1, stay2], [move1, move2]
        last = iteration == ITERS - 1
        for s in (1, 0):
            came = shifted(move[s], "tx", 1)
            below = stay[s][1] + came[1]
            above = stay[s][0] + came[0]
            from_above = shifted(below, "ty", 1)
            if last:
                own[s] = own[s] - step_size * (above + from_above)
                continue
            from_below = shifted(above, "ty", -1)
            own[s] = own[s] - step_size * (above + from_above)
            low[s] = low[s] - step_size * (from_below + below)
            rgt[s], dia[s] = shifted(own[s], "tx", -1), shifted(low[s], "tx", -1)
    return jnp.stack(own)


def solution(mesh):
    in_specs = (
        P(None, None, "ty", "tx"),
        P(),
        P(),
        P(None, "ty", "tx", None, None),
        P(None, "ty", "tx"),
        P(None, "ty", "tx", None, None, None),
    )
    out_specs = P(None, None, "ty", "tx")
    return jax.shard_map(shards, mesh=mesh, in_specs=in_specs, out_specs=out_specs, check_vma=False)
```

```python
import numpy as np

import jax
import jax.numpy as jnp
from jax import lax
from jax.experimental import pallas as pl
from jax.experimental.pallas import tpu as pltpu
from jax.sharding import PartitionSpec as P


ITERS = 2
SLOTS = 2
SIDE = 256
HALF = SIDE // 2

soft_floor = 0.01
step_size = 0.25


def dft_tables():
    k = np.arange(HALF)
    stack = []
    for parity in (0, 1):
        angle = 2.0 * np.pi * ((2 * k[:, None] + parity) * k[None, :] % SIDE) / SIDE
        cos, sin = np.cos(angle) / 16.0, np.sin(angle) / 16.0
        stack.append(np.block([[cos, sin], [-sin, cos]]))
    both = np.stack([np.stack(stack), np.stack([t.T for t in stack])])
    high = both.astype(jnp.bfloat16)
    low = (both - high.astype(np.float64)).astype(jnp.bfloat16)
    return np.stack([high, low], axis=2)


def shifted(value, axis, steps):
    count = lax.axis_size(axis)
    first, last = (max(0, -steps), min(count, count - steps))
    return lax.ppermute(value, axis, [(source, source + steps) for source in range(first, last)])


def split(value):
    high = value.astype(jnp.bfloat16)
    return high, (value - high.astype(jnp.float32)).astype(jnp.bfloat16)


def dot(left, right):
    return jnp.dot(left, right, preferred_element_type=jnp.float32)


def table_left(tables, flip, parity, value):
    high, low = split(value)
    t_high, t_low = tables[flip, parity, 0], tables[flip, parity, 1]
    return dot(t_high, high) + (dot(t_high, low) + dot(t_low, high))


def table_right(tables, flip, parity, value):
    high, low = split(value)
    t_high, t_low = tables[flip, parity, 0], tables[flip, parity, 1]
    return dot(high, t_high) + (dot(low, t_high) + dot(high, t_low))


def rows_cat(a, b):
    return jnp.concatenate([a, b], axis=0)


def lanes_cat(a, b):
    return jnp.concatenate([a, b], axis=1)


def forward(tables, re, im):
    ra, rb, ia, ib = re[:HALF], re[HALF:], im[:HALF], im[HALF:]
    even = table_left(tables, 0, 0, rows_cat(ra + rb, ia + ib))
    odd = table_left(tables, 0, 1, rows_cat(ra - rb, ia - ib))
    real = rows_cat(even[:HALF], odd[:HALF])
    imag = rows_cat(even[HALF:], odd[HALF:])
    ra, rb, ia, ib = real[:, :HALF], real[:, HALF:], imag[:, :HALF], imag[:, HALF:]
    return (
        table_right(tables, 1, 0, lanes_cat(ra + rb, ia + ib)),
        table_right(tables, 1, 1, lanes_cat(ra - rb, ia - ib)),
    )


def inverse(tables, even, odd):
    even = table_right(tables, 0, 0, even)
    odd = table_right(tables, 0, 1, odd)
    real = lanes_cat(even[:, :HALF] + odd[:, :HALF], even[:, :HALF] - odd[:, :HALF])
    imag = lanes_cat(even[:, HALF:] + odd[:, HALF:], even[:, HALF:] - odd[:, HALF:])
    even = table_left(tables, 1, 0, rows_cat(real[:HALF], imag[:HALF]))
    odd = table_left(tables, 1, 1, rows_cat(real[HALF:], imag[HALF:]))
    return (
        rows_cat(even[:HALF] + odd[:HALF], even[:HALF] - odd[:HALF]),
        rows_cat(even[HALF:] + odd[HALF:], even[HALF:] - odd[HALF:]),
    )


def masks(off_ref, iteration, slot):
    row = off_ref[iteration, slot, 0]
    col = off_ref[iteration, slot, 1]
    below = lax.broadcasted_iota(jnp.int32, (SIDE, SIDE), 0) < row
    right = lax.broadcasted_iota(jnp.int32, (SIDE, SIDE), 1) < col
    return below, right


def picked(below, right, own, rgt, low, dia, plane):
    upper = jnp.where(right, rgt[plane], own[plane])
    lower = jnp.where(right, dia[plane], low[plane])
    return jnp.where(below, lower, upper)


def placed(below, right, value, plane, stay, move):
    zero = jnp.zeros_like(value)
    left_part = jnp.where(right, zero, value)
    right_part = jnp.where(right, value, zero)
    stay[0, plane] += jnp.where(below, zero, left_part)
    stay[1, plane] += jnp.where(below, left_part, zero)
    move[0, plane] += jnp.where(below, zero, right_part)
    move[1, plane] += jnp.where(below, right_part, zero)


def prepare_kernel(off_ref, probe_ref, cos_ref, sin_ref, amp_ref, perm_ref,
                   rolled_ref, prop_ref, ampl_ref, twice):
    def reorder(src):
        rest = src[...]
        total = None
        for _ in range(3):
            part = rest.astype(jnp.bfloat16)
            rest = rest - part.astype(jnp.float32)
            part = dot(dot(perm_ref[0], part).astype(jnp.bfloat16), perm_ref[1])
            total = part if total is None else total + part
        return total

    def put(dst, value):
        dst[0] = value[:, :HALF]
        dst[1] = value[:, HALF:]

    def tile_loop(index, carry):
        it, slot = index // SLOTS, index % SLOTS
        row = off_ref[it, slot, 0]
        col = off_ref[it, slot, 1]
        for plane in range(2):
            start = pl.multiple_of(SIDE - 8 - row // 8 * 8, 8)
            turned = pltpu.roll(twice[plane, pl.ds(start, SIDE + 8), :], row % 8, 0)
            rolled_ref[it, slot, plane] = pltpu.roll(turned[8:], col, 1)
        put(ampl_ref.at[it, slot], reorder(amp_ref.at[it, slot]))
        return carry

    for plane in range(2):
        twice[plane, :SIDE] = probe_ref[plane]
        twice[plane, SIDE:] = probe_ref[plane]
    put(prop_ref.at[0], reorder(cos_ref))
    put(prop_ref.at[1], reorder(sin_ref))
    lax.fori_loop(0, ITERS * SLOTS, tile_loop, 0)


def first_kernel(iteration, off_ref, cnt_ref, own, rgt, low, dia, rolled, prop, tables, mid_ref):
    def body(slot, carry):
        below, right = masks(off_ref, iteration, slot)
        one_re = picked(below, right, own, rgt, low, dia, 0)
        one_im = picked(below, right, own, rgt, low, dia, 1)
        p_re, p_im = rolled[iteration, slot, 0], rolled[iteration, slot, 1]
        spec = forward(tables, p_re * one_re - p_im * one_im, p_re * one_im + p_im * one_re)
        moved = []
        for q in range(2):
            re, im = spec[q][:, :HALF], spec[q][:, HALF:]
            h_re, h_im = prop[0, q], prop[1, q]
            moved.append(lanes_cat(re * h_re - im * h_im, re * h_im + im * h_re))
        mid_ref[slot, 0], mid_ref[slot, 1] = inverse(tables, *moved)
        return carry

    lax.fori_loop(0, cnt_ref[iteration], body, 0)


def second_kernel(iteration, off_ref, cnt_ref, own, rgt, low, dia, mid_ref, ampl, tables,
                  stay, move, carry_ref):
    stay[...] = jnp.zeros_like(stay)
    move[...] = jnp.zeros_like(move)

    def body(slot, carry):
        below, right = masks(off_ref, iteration, slot)
        two_re = picked(below, right, own, rgt, low, dia, 0)
        two_im = picked(below, right, own, rgt, low, dia, 1)
        m_re, m_im = mid_ref[slot, 0], mid_ref[slot, 1]
        far = forward(tables, m_re * two_re - m_im * two_im, m_re * two_im + m_im * two_re)
        chi = []
        for q in range(2):
            re, im = far[q][:, :HALF], far[q][:, HALF:]
            factor = 1.0 - ampl[iteration, slot, q] * lax.rsqrt(re * re + im * im + soft_floor)
            chi.append(lanes_cat(re * factor, im * factor))
        b_re, b_im = inverse(tables, *chi)
        placed(below, right, m_re * b_re + m_im * b_im, 0, stay, move)
        placed(below, right, m_re * b_im - m_im * b_re, 1, stay, move)
        carry_ref[slot, 0] = two_re * b_re + two_im * b_im
        carry_ref[slot, 1] = two_re * b_im - two_im * b_re
        return carry

    lax.fori_loop(0, cnt_ref[iteration], body, 0)


def third_kernel(iteration, off_ref, cnt_ref, carry_ref, rolled, prop, tables, stay, move):
    stay[...] = jnp.zeros_like(stay)
    move[...] = jnp.zeros_like(move)

    def body(slot, carry):
        below, right = masks(off_ref, iteration, slot)
        spec = forward(tables, carry_ref[slot, 0], carry_ref[slot, 1])
        turned = []
        for q in range(2):
            re, im = spec[q][:, :HALF], spec[q][:, HALF:]
            h_re, h_im = prop[0, q], prop[1, q]
            turned.append(lanes_cat(re * h_re + im * h_im, im * h_re - re * h_im))
        e_re, e_im = inverse(tables, *turned)
        p_re, p_im = rolled[iteration, slot, 0], rolled[iteration, slot, 1]
        placed(below, right, p_re * e_re + p_im * e_im, 0, stay, move)
        placed(below, right, p_re * e_im - p_im * e_re, 1, stay, move)
        return carry

    lax.fori_loop(0, cnt_ref[iteration], body, 0)


SMEM = pl.BlockSpec(memory_space=pltpu.SMEM)
VMEM = pl.BlockSpec(memory_space=pltpu.VMEM)
LIMIT = 24 * 1024 * 1024


def f32(*shape):
    return jax.ShapeDtypeStruct(shape, jnp.float32)


def call(body, scalars, arrays, outs, scratch=()):
    args = [*scalars, *arrays]
    return pl.pallas_call(
        body,
        out_shape=outs,
        in_specs=[SMEM] * len(scalars) + [VMEM] * len(arrays),
        out_specs=[VMEM] * len(outs),
        scratch_shapes=scratch,
        compiler_params=pltpu.CompilerParams(vmem_limit_bytes=LIMIT),
        cost_estimate=pl.CostEstimate(flops=4 * 10**9, bytes_accessed=8 * 2**20, transcendentals=0),
    )(*args)


def shards(object_tiles, probe_field, prop_angle, scan_offsets, probe_counts, amplitudes):
    tables = jnp.asarray(dft_tables())
    lane = np.arange(SIDE)
    source = np.concatenate([lane[0::2], lane[1::2]])
    perm = np.zeros((SIDE, SIDE), np.float32)
    perm[source, lane] = 1.0
    perm = jnp.asarray(np.stack([perm.T, perm]).astype(jnp.bfloat16))
    offsets = scan_offsets.reshape(ITERS, SLOTS, 2)
    counts = probe_counts.reshape(ITERS)
    measured = amplitudes.reshape(ITERS, SLOTS, SIDE, SIDE)

    own = [object_tiles[0], object_tiles[1]]
    low, rgt, dia = [None, None], [None, None], [None, None]
    for s in (0, 1):
        low[s] = shifted(own[s], "ty", -1)
        rgt[s] = shifted(own[s], "tx", -1)
    for s in (0, 1):
        dia[s] = shifted(low[s], "tx", -1)

    rolled, prop, ampl = call(
        prepare_kernel, [offsets],
        [probe_field, jnp.cos(prop_angle), jnp.sin(prop_angle), measured, perm],
        [f32(ITERS, SLOTS, 2, SIDE, SIDE), f32(2, 2, SIDE, HALF), f32(ITERS, SLOTS, 2, SIDE, HALF)],
        [pltpu.VMEM((2, 2 * SIDE, SIDE), jnp.float32)],
    )
    pair = f32(2, 2, SIDE, SIDE)

    for iteration in range(ITERS):
        def bind(kernel, iteration=iteration):
            return lambda *refs: kernel(iteration, *refs)

        scalars = [offsets, counts]
        (mid,) = call(bind(first_kernel), scalars,
                      [own[0], rgt[0], low[0], dia[0], rolled, prop, tables], [pair])
        stay2, move2, carry = call(bind(second_kernel), scalars,
                                   [own[1], rgt[1], low[1], dia[1], mid, ampl, tables], [pair] * 3)
        stay1, move1 = call(bind(third_kernel), scalars,
                            [carry, rolled, prop, tables], [pair] * 2)
        stay, move = [stay1, stay2], [move1, move2]
        last = iteration == ITERS - 1
        came, above, below = [None, None], [None, None], [None, None]
        for s in (1, 0):
            came[s] = shifted(move[s], "tx", 1)
            sums = (stay[s][0] + came[s][0], stay[s][1] + came[s][1])
            above[s], below[s] = lax.optimization_barrier(sums)
        for s in (1, 0):
            from_above = shifted(below[s], "ty", 1)
            if last:
                own[s] = own[s] - step_size * (above[s] + from_above)
                continue
            from_below = shifted(above[s], "ty", -1)
            own[s] = own[s] - step_size * (above[s] + from_above)
            low[s] = low[s] - step_size * (from_below + below[s])
            both = shifted(jnp.stack([own[s], low[s]]), "tx", -1)
            rgt[s], dia[s] = both[0], both[1]
    return jnp.stack(own)


def solution(mesh):
    in_specs = (
        P(None, None, "ty", "tx"),
        P(),
        P(),
        P(None, "ty", "tx", None, None),
        P(None, "ty", "tx"),
        P(None, "ty", "tx", None, None, None),
    )
    out_specs = P(None, None, "ty", "tx")

    return jax.shard_map(shards, mesh=mesh, in_specs=in_specs, out_specs=out_specs, check_vma=False)
```

```python
import numpy as np

import jax
import jax.numpy as jnp
from jax import lax
from jax.experimental import pallas as pl
from jax.experimental.pallas import tpu as pltpu
from jax.sharding import PartitionSpec as P


ITERS = 2
SLOTS = 2
SIDE = 256
HALF = SIDE // 2

soft_floor = 0.01
step_size = 0.25


def dft_tables():
    k = np.arange(HALF)
    stack = []
    for parity in (0, 1):
        angle = 2.0 * np.pi * ((2 * k[:, None] + parity) * k[None, :] % SIDE) / SIDE
        cos, sin = np.cos(angle) / 16.0, np.sin(angle) / 16.0
        stack.append(np.block([[cos, sin], [-sin, cos]]))
    both = np.stack([np.stack(stack), np.stack([t.T for t in stack])])
    high = both.astype(jnp.bfloat16)
    low = (both - high.astype(np.float64)).astype(jnp.bfloat16)
    return np.stack([high, low], axis=2)


def shifted(value, axis, steps):
    count = lax.axis_size(axis)
    first, last = (max(0, -steps), min(count, count - steps))
    return lax.ppermute(value, axis, [(source, source + steps) for source in range(first, last)])


def split(value):
    high = value.astype(jnp.bfloat16)
    return high, (value - high.astype(jnp.float32)).astype(jnp.bfloat16)


def dot(left, right):
    return jnp.dot(left, right, preferred_element_type=jnp.float32)


def table_left(tables, flip, parity, value):
    high, low = split(value)
    t_high, t_low = tables[flip, parity, 0], tables[flip, parity, 1]
    return dot(t_high, high) + (dot(t_high, low) + dot(t_low, high))


def table_right(tables, flip, parity, value):
    high, low = split(value)
    t_high, t_low = tables[flip, parity, 0], tables[flip, parity, 1]
    return dot(high, t_high) + (dot(low, t_high) + dot(high, t_low))


def rows_cat(a, b):
    return jnp.concatenate([a, b], axis=0)


def lanes_cat(a, b):
    return jnp.concatenate([a, b], axis=1)


def forward(tables, re, im):
    ra, rb, ia, ib = re[:HALF], re[HALF:], im[:HALF], im[HALF:]
    even = table_left(tables, 0, 0, rows_cat(ra + rb, ia + ib))
    odd = table_left(tables, 0, 1, rows_cat(ra - rb, ia - ib))
    real = rows_cat(even[:HALF], odd[:HALF])
    imag = rows_cat(even[HALF:], odd[HALF:])
    ra, rb, ia, ib = real[:, :HALF], real[:, HALF:], imag[:, :HALF], imag[:, HALF:]
    return (
        table_right(tables, 1, 0, lanes_cat(ra + rb, ia + ib)),
        table_right(tables, 1, 1, lanes_cat(ra - rb, ia - ib)),
    )


def inverse(tables, even, odd):
    even = table_right(tables, 0, 0, even)
    odd = table_right(tables, 0, 1, odd)
    real = lanes_cat(even[:, :HALF] + odd[:, :HALF], even[:, :HALF] - odd[:, :HALF])
    imag = lanes_cat(even[:, HALF:] + odd[:, HALF:], even[:, HALF:] - odd[:, HALF:])
    even = table_left(tables, 1, 0, rows_cat(real[:HALF], imag[:HALF]))
    odd = table_left(tables, 1, 1, rows_cat(real[HALF:], imag[HALF:]))
    return (
        rows_cat(even[:HALF] + odd[:HALF], even[:HALF] - odd[:HALF]),
        rows_cat(even[HALF:] + odd[HALF:], even[HALF:] - odd[HALF:]),
    )


def four(tiles):
    if len(tiles) == 4:
        return tiles
    mine, theirs = tiles
    return mine.at[0], theirs.at[0], mine.at[1], theirs.at[1]


def masks(off_ref, iteration, slot):
    row = off_ref[iteration, slot, 0]
    col = off_ref[iteration, slot, 1]
    below = lax.broadcasted_iota(jnp.int32, (SIDE, SIDE), 0) < row
    right = lax.broadcasted_iota(jnp.int32, (SIDE, SIDE), 1) < col
    return below, right


def picked(below, right, own, rgt, low, dia, plane):
    upper = jnp.where(right, rgt[plane], own[plane])
    lower = jnp.where(right, dia[plane], low[plane])
    return jnp.where(below, lower, upper)


def placed(below, right, value, plane, stay, move):
    zero = jnp.zeros_like(value)
    left_part = jnp.where(right, zero, value)
    right_part = jnp.where(right, value, zero)
    stay[0, plane] += jnp.where(below, zero, left_part)
    stay[1, plane] += jnp.where(below, left_part, zero)
    move[0, plane] += jnp.where(below, zero, right_part)
    move[1, plane] += jnp.where(below, right_part, zero)


def prepare_kernel(off_ref, probe_ref, cos_ref, sin_ref, amp_ref, perm_ref,
                   rolled_ref, prop_ref, ampl_ref, twice):
    def reorder(src):
        rest = src[...]
        total = None
        for _ in range(3):
            part = rest.astype(jnp.bfloat16)
            rest = rest - part.astype(jnp.float32)
            part = dot(dot(perm_ref[0], part).astype(jnp.bfloat16), perm_ref[1])
            total = part if total is None else total + part
        return total

    def put(dst, value):
        dst[0] = value[:, :HALF]
        dst[1] = value[:, HALF:]

    def tile_loop(index, carry):
        it, slot = index // SLOTS, index % SLOTS
        row = off_ref[it, slot, 0]
        col = off_ref[it, slot, 1]
        for plane in range(2):
            start = pl.multiple_of(SIDE - 8 - row // 8 * 8, 8)
            turned = pltpu.roll(twice[plane, pl.ds(start, SIDE + 8), :], row % 8, 0)
            rolled_ref[it, slot, plane] = pltpu.roll(turned[8:], col, 1)
        put(ampl_ref.at[it, slot], reorder(amp_ref.at[it, slot]))
        return carry

    for plane in range(2):
        twice[plane, :SIDE] = probe_ref[plane]
        twice[plane, SIDE:] = probe_ref[plane]
    put(prop_ref.at[0], reorder(cos_ref))
    put(prop_ref.at[1], reorder(sin_ref))
    lax.fori_loop(0, ITERS * SLOTS, tile_loop, 0)


def first_kernel(iteration, off_ref, cnt_ref, rolled, prop, tables, *refs):
    *tiles, mid_ref = refs
    own, rgt, low, dia = four(tiles)

    def body(slot, carry):
        below, right = masks(off_ref, iteration, slot)
        one_re = picked(below, right, own, rgt, low, dia, 0)
        one_im = picked(below, right, own, rgt, low, dia, 1)
        p_re, p_im = rolled[iteration, slot, 0], rolled[iteration, slot, 1]
        spec = forward(tables, p_re * one_re - p_im * one_im, p_re * one_im + p_im * one_re)
        moved = []
        for q in range(2):
            re, im = spec[q][:, :HALF], spec[q][:, HALF:]
            h_re, h_im = prop[0, q], prop[1, q]
            moved.append(lanes_cat(re * h_re - im * h_im, re * h_im + im * h_re))
        mid_ref[slot, 0], mid_ref[slot, 1] = inverse(tables, *moved)
        return carry

    lax.fori_loop(0, cnt_ref[iteration], body, 0)


def second_kernel(iteration, off_ref, cnt_ref, mid_ref, ampl, tables, *refs):
    *tiles, stay, move, carry_ref = refs
    own, rgt, low, dia = four(tiles)
    stay[...] = jnp.zeros_like(stay)
    move[...] = jnp.zeros_like(move)

    def body(slot, carry):
        below, right = masks(off_ref, iteration, slot)
        two_re = picked(below, right, own, rgt, low, dia, 0)
        two_im = picked(below, right, own, rgt, low, dia, 1)
        m_re, m_im = mid_ref[slot, 0], mid_ref[slot, 1]
        far = forward(tables, m_re * two_re - m_im * two_im, m_re * two_im + m_im * two_re)
        chi = []
        for q in range(2):
            re, im = far[q][:, :HALF], far[q][:, HALF:]
            factor = 1.0 - ampl[iteration, slot, q] * lax.rsqrt(re * re + im * im + soft_floor)
            chi.append(lanes_cat(re * factor, im * factor))
        b_re, b_im = inverse(tables, *chi)
        placed(below, right, m_re * b_re + m_im * b_im, 0, stay, move)
        placed(below, right, m_re * b_im - m_im * b_re, 1, stay, move)
        carry_ref[slot, 0] = two_re * b_re + two_im * b_im
        carry_ref[slot, 1] = two_re * b_im - two_im * b_re
        return carry

    lax.fori_loop(0, cnt_ref[iteration], body, 0)


def third_kernel(iteration, off_ref, cnt_ref, carry_ref, rolled, prop, tables, stay, move):
    stay[...] = jnp.zeros_like(stay)
    move[...] = jnp.zeros_like(move)

    def body(slot, carry):
        below, right = masks(off_ref, iteration, slot)
        spec = forward(tables, carry_ref[slot, 0], carry_ref[slot, 1])
        turned = []
        for q in range(2):
            re, im = spec[q][:, :HALF], spec[q][:, HALF:]
            h_re, h_im = prop[0, q], prop[1, q]
            turned.append(lanes_cat(re * h_re + im * h_im, im * h_re - re * h_im))
        e_re, e_im = inverse(tables, *turned)
        p_re, p_im = rolled[iteration, slot, 0], rolled[iteration, slot, 1]
        placed(below, right, p_re * e_re + p_im * e_im, 0, stay, move)
        placed(below, right, p_re * e_im - p_im * e_re, 1, stay, move)
        return carry

    lax.fori_loop(0, cnt_ref[iteration], body, 0)


def update_kernel(above, below, from_above, from_below, *refs):
    *tiles, mine = refs
    mine[0] = tiles[0][...] - step_size * (above[...] + from_above[...])
    mine[1] = tiles[1][...] - step_size * (from_below[...] + below[...])


def last_kernel(one, two, above1, above2, from_above1, from_above2, out):
    out[0] = one[0] - step_size * (above1[...] + from_above1[...])
    out[1] = two[0] - step_size * (above2[...] + from_above2[...])


SMEM = pl.BlockSpec(memory_space=pltpu.SMEM)
VMEM = pl.BlockSpec(memory_space=pltpu.VMEM)
LIMIT = 24 * 1024 * 1024


def f32(*shape):
    return jax.ShapeDtypeStruct(shape, jnp.float32)


def call(body, scalars, arrays, outs, scratch=(), flops=4 * 10**9):
    args = [*scalars, *arrays]
    return pl.pallas_call(
        body,
        out_shape=outs,
        in_specs=[SMEM] * len(scalars) + [VMEM] * len(arrays),
        out_specs=[VMEM] * len(outs),
        scratch_shapes=scratch,
        compiler_params=pltpu.CompilerParams(vmem_limit_bytes=LIMIT),
        cost_estimate=pl.CostEstimate(flops=flops, bytes_accessed=8 * 2**20, transcendentals=0),
    )(*args)


def shards(object_tiles, probe_field, prop_angle, scan_offsets, probe_counts, amplitudes):
    tables = jnp.asarray(dft_tables())
    lane = np.arange(SIDE)
    source = np.concatenate([lane[0::2], lane[1::2]])
    perm = np.zeros((SIDE, SIDE), np.float32)
    perm[source, lane] = 1.0
    perm = jnp.asarray(np.stack([perm.T, perm]).astype(jnp.bfloat16))
    offsets = scan_offsets.reshape(ITERS, SLOTS, 2)
    counts = probe_counts.reshape(ITERS)
    measured = amplitudes.reshape(ITERS, SLOTS, SIDE, SIDE)

    own = [object_tiles[0], object_tiles[1]]
    low, rgt, dia = [None, None], [None, None], [None, None]
    for s in (0, 1):
        low[s] = shifted(own[s], "ty", -1)
        rgt[s] = shifted(own[s], "tx", -1)
    for s in (0, 1):
        dia[s] = shifted(low[s], "tx", -1)

    rolled, prop, ampl = call(
        prepare_kernel, [offsets],
        [probe_field, jnp.cos(prop_angle), jnp.sin(prop_angle), measured, perm],
        [f32(ITERS, SLOTS, 2, SIDE, SIDE), f32(2, 2, SIDE, HALF), f32(ITERS, SLOTS, 2, SIDE, HALF)],
        [pltpu.VMEM((2, 2 * SIDE, SIDE), jnp.float32)],
    )
    pair = f32(2, 2, SIDE, SIDE)

    tiles = [[own[s], rgt[s], low[s], dia[s]] for s in (0, 1)]

    for iteration in range(ITERS):
        def bind(kernel, iteration=iteration):
            return lambda *refs: kernel(iteration, *refs)

        scalars = [offsets, counts]
        (mid,) = call(bind(first_kernel), scalars, [rolled, prop, tables, *tiles[0]], [pair])
        stay2, move2, carry = call(bind(second_kernel), scalars,
                                   [mid, ampl, tables, *tiles[1]], [pair] * 3)
        stay1, move1 = call(bind(third_kernel), scalars,
                            [carry, rolled, prop, tables], [pair] * 2)
        stay, move = [stay1, stay2], [move1, move2]
        above, below, came = [None, None], [None, None], [None, None]
        for s in (1, 0):
            came[s] = shifted(move[s], "tx", 1)
            sums = (stay[s][0] + came[s][0], stay[s][1] + came[s][1])
            above[s], below[s] = lax.optimization_barrier(sums)
        from_above = [None, None]
        for s in (1, 0):
            from_above[s] = shifted(below[s], "ty", 1)
            if iteration == ITERS - 1:
                continue
            from_below = shifted(above[s], "ty", -1)
            held = [tiles[s][0], tiles[s][2]]
            (mine,) = call(update_kernel, [],
                           [above[s], below[s], from_above[s], from_below, *held], [pair], flops=10**6)
            tiles[s] = [mine, shifted(mine, "tx", -1)]
    (out,) = call(last_kernel, [], [tiles[0][0], tiles[1][0], *above, *from_above], [pair], flops=10**6)
    return out


def solution(mesh):
    in_specs = (
        P(None, None, "ty", "tx"),
        P(),
        P(),
        P(None, "ty", "tx", None, None),
        P(None, "ty", "tx"),
        P(None, "ty", "tx", None, None, None),
    )
    out_specs = P(None, None, "ty", "tx")

    return jax.shard_map(shards, mesh=mesh, in_specs=in_specs, out_specs=out_specs, check_vma=False)
```

```python
import numpy as np

import jax
import jax.numpy as jnp
from jax import lax
from jax.experimental import pallas as pl
from jax.experimental.pallas import tpu as pltpu
from jax.sharding import PartitionSpec as P


ITERS = 2
SLOTS = 2
SIDE = 256
HALF = SIDE // 2

soft_floor = 0.01
step_size = 0.25


def dft_tables():
    k = np.arange(HALF)
    stack = []
    for parity in (0, 1):
        angle = 2.0 * np.pi * ((2 * k[:, None] + parity) * k[None, :] % SIDE) / SIDE
        cos, sin = np.cos(angle) / 16.0, np.sin(angle) / 16.0
        stack.append(np.block([[cos, sin], [-sin, cos]]))
    both = np.stack([np.stack(stack), np.stack([t.T for t in stack])])
    high = both.astype(jnp.bfloat16)
    low = (both - high.astype(np.float64)).astype(jnp.bfloat16)
    return np.stack([high, low], axis=2)


def shifted(value, axis, steps):
    count = lax.axis_size(axis)
    first, last = (max(0, -steps), min(count, count - steps))
    return lax.ppermute(value, axis, [(source, source + steps) for source in range(first, last)])


def around(value, steps, sizes):
    rows, cols = sizes
    first, second = [], []
    for row in range(max(0, -steps), min(rows, rows - steps)):
        for col in range(cols):
            z = (2 * (row % 4) + col // 2 % 2 - 3 * steps) % 8
            relay = (row // 4 * 4 + z // 2) * cols + col // 4 * 4 + z % 2 * 2 + col % 2
            first.append((row * cols + col, relay))
            second.append((relay, (row + steps) * cols + col))
    value = lax.ppermute(value, ("ty", "tx"), first)
    return lax.ppermute(value, ("ty", "tx"), second)


def split(value):
    high = value.astype(jnp.bfloat16)
    return high, (value - high.astype(jnp.float32)).astype(jnp.bfloat16)


def dot(left, right):
    return jnp.dot(left, right, preferred_element_type=jnp.float32)


def table_left(tables, flip, parity, value):
    high, low = split(value)
    t_high, t_low = tables[flip, parity, 0], tables[flip, parity, 1]
    return dot(t_high, high) + (dot(t_high, low) + dot(t_low, high))


def table_right(tables, flip, parity, value):
    high, low = split(value)
    t_high, t_low = tables[flip, parity, 0], tables[flip, parity, 1]
    return dot(high, t_high) + (dot(low, t_high) + dot(high, t_low))


def rows_cat(a, b):
    return jnp.concatenate([a, b], axis=0)


def lanes_cat(a, b):
    return jnp.concatenate([a, b], axis=1)


def forward(tables, re, im):
    ra, rb, ia, ib = re[:HALF], re[HALF:], im[:HALF], im[HALF:]
    even = table_left(tables, 0, 0, rows_cat(ra + rb, ia + ib))
    odd = table_left(tables, 0, 1, rows_cat(ra - rb, ia - ib))
    real = rows_cat(even[:HALF], odd[:HALF])
    imag = rows_cat(even[HALF:], odd[HALF:])
    ra, rb, ia, ib = real[:, :HALF], real[:, HALF:], imag[:, :HALF], imag[:, HALF:]
    return (
        table_right(tables, 1, 0, lanes_cat(ra + rb, ia + ib)),
        table_right(tables, 1, 1, lanes_cat(ra - rb, ia - ib)),
    )


def inverse(tables, even, odd):
    even = table_right(tables, 0, 0, even)
    odd = table_right(tables, 0, 1, odd)
    real = lanes_cat(even[:, :HALF] + odd[:, :HALF], even[:, :HALF] - odd[:, :HALF])
    imag = lanes_cat(even[:, HALF:] + odd[:, HALF:], even[:, HALF:] - odd[:, HALF:])
    even = table_left(tables, 1, 0, rows_cat(real[:HALF], imag[:HALF]))
    odd = table_left(tables, 1, 1, rows_cat(real[HALF:], imag[HALF:]))
    return (
        rows_cat(even[:HALF] + odd[:HALF], even[:HALF] - odd[:HALF]),
        rows_cat(even[HALF:] + odd[HALF:], even[HALF:] - odd[HALF:]),
    )


def four(tiles):
    if len(tiles) == 4:
        return tiles
    mine, theirs = tiles
    return mine.at[0], theirs.at[0], mine.at[1], theirs.at[1]


def masks(off_ref, iteration, slot):
    row = off_ref[iteration, slot, 0]
    col = off_ref[iteration, slot, 1]
    below = lax.broadcasted_iota(jnp.int32, (SIDE, SIDE), 0) < row
    right = lax.broadcasted_iota(jnp.int32, (SIDE, SIDE), 1) < col
    return below, right


def picked(below, right, own, rgt, low, dia, plane):
    upper = jnp.where(right, rgt[plane], own[plane])
    lower = jnp.where(right, dia[plane], low[plane])
    return jnp.where(below, lower, upper)


def placed(below, right, value, plane, stay, move):
    zero = jnp.zeros_like(value)
    left_part = jnp.where(right, zero, value)
    right_part = jnp.where(right, value, zero)
    stay[0, plane] += jnp.where(below, zero, left_part)
    stay[1, plane] += jnp.where(below, left_part, zero)
    move[0, plane] += jnp.where(below, zero, right_part)
    move[1, plane] += jnp.where(below, right_part, zero)


def prepare_kernel(off_ref, probe_ref, cos_ref, sin_ref, amp_ref, perm_ref,
                   rolled_ref, prop_ref, ampl_ref, twice):
    def reorder(src):
        rest = src[...]
        total = None
        for _ in range(3):
            part = rest.astype(jnp.bfloat16)
            rest = rest - part.astype(jnp.float32)
            part = dot(dot(perm_ref[0], part).astype(jnp.bfloat16), perm_ref[1])
            total = part if total is None else total + part
        return total

    def put(dst, value):
        dst[0] = value[:, :HALF]
        dst[1] = value[:, HALF:]

    def tile_loop(index, carry):
        it, slot = index // SLOTS, index % SLOTS
        row = off_ref[it, slot, 0]
        col = off_ref[it, slot, 1]
        for plane in range(2):
            start = pl.multiple_of(SIDE - 8 - row // 8 * 8, 8)
            turned = pltpu.roll(twice[plane, pl.ds(start, SIDE + 8), :], row % 8, 0)
            rolled_ref[it, slot, plane] = pltpu.roll(turned[8:], col, 1)
        put(ampl_ref.at[it, slot], reorder(amp_ref.at[it, slot]))
        return carry

    for plane in range(2):
        twice[plane, :SIDE] = probe_ref[plane]
        twice[plane, SIDE:] = probe_ref[plane]
    put(prop_ref.at[0], reorder(cos_ref))
    put(prop_ref.at[1], reorder(sin_ref))
    lax.fori_loop(0, ITERS * SLOTS, tile_loop, 0)


def first_kernel(iteration, off_ref, cnt_ref, rolled, prop, tables, *refs):
    *tiles, mid_ref = refs
    own, rgt, low, dia = four(tiles)

    def body(slot, carry):
        below, right = masks(off_ref, iteration, slot)
        one_re = picked(below, right, own, rgt, low, dia, 0)
        one_im = picked(below, right, own, rgt, low, dia, 1)
        p_re, p_im = rolled[iteration, slot, 0], rolled[iteration, slot, 1]
        spec = forward(tables, p_re * one_re - p_im * one_im, p_re * one_im + p_im * one_re)
        moved = []
        for q in range(2):
            re, im = spec[q][:, :HALF], spec[q][:, HALF:]
            h_re, h_im = prop[0, q], prop[1, q]
            moved.append(lanes_cat(re * h_re - im * h_im, re * h_im + im * h_re))
        mid_ref[slot, 0], mid_ref[slot, 1] = inverse(tables, *moved)
        return carry

    lax.fori_loop(0, cnt_ref[iteration], body, 0)


def second_kernel(iteration, off_ref, cnt_ref, mid_ref, ampl, tables, *refs):
    *tiles, stay, move, carry_ref = refs
    own, rgt, low, dia = four(tiles)
    stay[...] = jnp.zeros_like(stay)
    move[...] = jnp.zeros_like(move)

    def body(slot, carry):
        below, right = masks(off_ref, iteration, slot)
        two_re = picked(below, right, own, rgt, low, dia, 0)
        two_im = picked(below, right, own, rgt, low, dia, 1)
        m_re, m_im = mid_ref[slot, 0], mid_ref[slot, 1]
        far = forward(tables, m_re * two_re - m_im * two_im, m_re * two_im + m_im * two_re)
        chi = []
        for q in range(2):
            re, im = far[q][:, :HALF], far[q][:, HALF:]
            factor = 1.0 - ampl[iteration, slot, q] * lax.rsqrt(re * re + im * im + soft_floor)
            chi.append(lanes_cat(re * factor, im * factor))
        b_re, b_im = inverse(tables, *chi)
        placed(below, right, m_re * b_re + m_im * b_im, 0, stay, move)
        placed(below, right, m_re * b_im - m_im * b_re, 1, stay, move)
        carry_ref[slot, 0] = two_re * b_re + two_im * b_im
        carry_ref[slot, 1] = two_re * b_im - two_im * b_re
        return carry

    lax.fori_loop(0, cnt_ref[iteration], body, 0)


def third_kernel(iteration, off_ref, cnt_ref, carry_ref, rolled, prop, tables, stay, move):
    stay[...] = jnp.zeros_like(stay)
    move[...] = jnp.zeros_like(move)

    def body(slot, carry):
        below, right = masks(off_ref, iteration, slot)
        spec = forward(tables, carry_ref[slot, 0], carry_ref[slot, 1])
        turned = []
        for q in range(2):
            re, im = spec[q][:, :HALF], spec[q][:, HALF:]
            h_re, h_im = prop[0, q], prop[1, q]
            turned.append(lanes_cat(re * h_re + im * h_im, im * h_re - re * h_im))
        e_re, e_im = inverse(tables, *turned)
        p_re, p_im = rolled[iteration, slot, 0], rolled[iteration, slot, 1]
        placed(below, right, p_re * e_re + p_im * e_im, 0, stay, move)
        placed(below, right, p_re * e_im - p_im * e_re, 1, stay, move)
        return carry

    lax.fori_loop(0, cnt_ref[iteration], body, 0)


def update_kernel(above, below, from_above, from_below, *refs):
    *tiles, mine = refs
    mine[0] = tiles[0][...] - step_size * (above[...] + from_above[...])
    mine[1] = tiles[1][...] - step_size * (from_below[...] + below[...])


def sums_kernel(stay, came, above, *below):
    above[...] = stay[0] + came[0]
    if len(below) == 1:
        below[0][...] = stay[1] + came[1]
    else:
        for plane in range(2):
            below[plane][...] = stay[1, plane] + came[1, plane]


def last_kernel(one, two, above1, above2, near2, far2, from_above1, out):
    out[0] = one[0] - step_size * (above1[...] + from_above1[...])
    out[1, 0] = two[0, 0] - step_size * (above2[0] + near2[...])
    out[1, 1] = two[0, 1] - step_size * (above2[1] + far2[...])


SMEM = pl.BlockSpec(memory_space=pltpu.SMEM)
VMEM = pl.BlockSpec(memory_space=pltpu.VMEM)
LIMIT = 24 * 1024 * 1024


def f32(*shape):
    return jax.ShapeDtypeStruct(shape, jnp.float32)


def call(body, scalars, arrays, outs, scratch=(), flops=4 * 10**9):
    args = [*scalars, *arrays]
    return pl.pallas_call(
        body,
        out_shape=outs,
        in_specs=[SMEM] * len(scalars) + [VMEM] * len(arrays),
        out_specs=[VMEM] * len(outs),
        scratch_shapes=scratch,
        compiler_params=pltpu.CompilerParams(vmem_limit_bytes=LIMIT),
        cost_estimate=pl.CostEstimate(flops=flops, bytes_accessed=8 * 2**20, transcendentals=0),
    )(*args)


def shards(object_tiles, probe_field, prop_angle, scan_offsets, probe_counts, amplitudes):
    tables = jnp.asarray(dft_tables())
    lane = np.arange(SIDE)
    source = np.concatenate([lane[0::2], lane[1::2]])
    perm = np.zeros((SIDE, SIDE), np.float32)
    perm[source, lane] = 1.0
    perm = jnp.asarray(np.stack([perm.T, perm]).astype(jnp.bfloat16))
    offsets = scan_offsets.reshape(ITERS, SLOTS, 2)
    counts = probe_counts.reshape(ITERS)
    measured = amplitudes.reshape(ITERS, SLOTS, SIDE, SIDE)

    sizes = lax.axis_size("ty"), lax.axis_size("tx")
    own = [object_tiles[0], object_tiles[1]]
    low0 = shifted(own[0], "ty", -1)
    far = around(object_tiles[1, 1], -1, sizes)
    rgt = [shifted(own[s], "tx", -1) for s in (0, 1)]
    near = shifted(object_tiles[1, 0], "ty", -1)
    low = [low0, jnp.stack([near, far])]
    dia = [shifted(low[s], "tx", -1) for s in (0, 1)]

    rolled, prop, ampl = call(
        prepare_kernel, [offsets],
        [probe_field, jnp.cos(prop_angle), jnp.sin(prop_angle), measured, perm],
        [f32(ITERS, SLOTS, 2, SIDE, SIDE), f32(2, 2, SIDE, HALF), f32(ITERS, SLOTS, 2, SIDE, HALF)],
        [pltpu.VMEM((2, 2 * SIDE, SIDE), jnp.float32)],
    )
    pair = f32(2, 2, SIDE, SIDE)

    tiles = [[own[s], rgt[s], low[s], dia[s]] for s in (0, 1)]

    for iteration in range(ITERS):
        def bind(kernel, iteration=iteration):
            return lambda *refs: kernel(iteration, *refs)

        scalars = [offsets, counts]
        (mid,) = call(bind(first_kernel), scalars, [rolled, prop, tables, *tiles[0]], [pair])
        stay2, move2, carry = call(bind(second_kernel), scalars,
                                   [mid, ampl, tables, *tiles[1]], [pair] * 3)
        stay1, move1 = call(bind(third_kernel), scalars,
                            [carry, rolled, prop, tables], [pair] * 2)
        stay, move = [stay1, stay2], [move1, move2]
        above, below, came, from_above = [None, None], [None, None], [None, None], []
        last = iteration == ITERS - 1
        for s in (1, 0):
            came[s] = shifted(move[s], "tx", 1)
            cut = last and s == 1
            outs = [f32(2, SIDE, SIDE)] + ([f32(SIDE, SIDE)] * 2 if cut else [f32(2, SIDE, SIDE)])
            above[s], *below[s] = call(sums_kernel, [], [stay[s], came[s]], outs, flops=10**6)
        for s in (1, 0):
            if last and s == 1:
                far = around(below[s][1], 1, sizes)
                from_above += [shifted(below[s][0], "ty", 1), far]
                continue
            fallen = shifted(below[s][0], "ty", 1)
            if last:
                from_above.append(fallen)
                continue
            from_below = shifted(above[s], "ty", -1)
            held = [tiles[s][0], tiles[s][2]]
            (mine,) = call(update_kernel, [],
                           [above[s], below[s][0], fallen, from_below, *held], [pair], flops=10**6)
            tiles[s] = [mine, shifted(mine, "tx", -1)]
    (out,) = call(last_kernel, [], [tiles[0][0], tiles[1][0], *above, *from_above], [pair], flops=10**6)
    return out


def solution(mesh):
    in_specs = (
        P(None, None, "ty", "tx"),
        P(),
        P(),
        P(None, "ty", "tx", None, None),
        P(None, "ty", "tx"),
        P(None, "ty", "tx", None, None, None),
    )
    out_specs = P(None, None, "ty", "tx")

    return jax.shard_map(shards, mesh=mesh, in_specs=in_specs, out_specs=out_specs, check_vma=False)
```

```python
import numpy as np

import jax
import jax.numpy as jnp
from jax import lax
from jax.experimental import pallas as pl
from jax.experimental.pallas import tpu as pltpu
from jax.sharding import PartitionSpec as P


ITERS = 2
SLOTS = 2
SIDE = 256
HALF = SIDE // 2

soft_floor = 0.01
step_size = 0.25


def dft_tables():
    k = np.arange(HALF)
    stack = []
    for parity in (0, 1):
        angle = 2.0 * np.pi * ((2 * k[:, None] + parity) * k[None, :] % SIDE) / SIDE
        cos, sin = np.cos(angle) / 16.0, np.sin(angle) / 16.0
        stack.append(np.block([[cos, sin], [-sin, cos]]))
    both = np.stack([np.stack(stack), np.stack([t.T for t in stack])])
    high = both.astype(jnp.bfloat16)
    low = (both - high.astype(np.float64)).astype(jnp.bfloat16)
    return np.stack([high, low], axis=2)


def shifted(value, axis, steps):
    count = lax.axis_size(axis)
    first, last = (max(0, -steps), min(count, count - steps))
    return lax.ppermute(value, axis, [(source, source + steps) for source in range(first, last)])


def moved(value, target, sizes):
    rows, cols = sizes
    pairs = []
    for row in range(rows):
        for col in range(cols):
            new_row, new_col = target(row, col)
            if 0 <= new_row < rows and 0 <= new_col < cols:
                pairs.append((row * cols + col, new_row * cols + new_col))
    return lax.ppermute(value, ("ty", "tx"), pairs)


NOWHERE = (-1, -1)


def diagonal_back(row, col):
    return (row - 1, col - 1) if col % 4 == 0 else (row, col - 1)


def diagonal_on(row, col):
    return (row + 1, col + 1) if col % 4 == 3 else (row, col + 1)


def around(value, steps, sizes):
    rows, cols = sizes

    def relay(row, col):
        z = (2 * (row % 4) + col // 2 % 2 - 3 * steps) % 8
        return row // 4 * 4 + z // 2, col // 4 * 4 + z % 2 * 2 + col % 2

    spots = [(r, c) for r in range(rows) for c in range(cols) if 0 <= r + steps < rows]
    ends = {relay(*spot): (spot[0] + steps, spot[1]) for spot in spots}
    value = moved(value, lambda r, c: relay(r, c) if (r, c) in spots else NOWHERE, sizes)
    return moved(value, lambda r, c: ends.get((r, c), NOWHERE), sizes)


def split(value):
    high = value.astype(jnp.bfloat16)
    return high, (value - high.astype(jnp.float32)).astype(jnp.bfloat16)


def dot(left, right):
    return jnp.dot(left, right, preferred_element_type=jnp.float32)


def table_left(tables, flip, parity, value):
    high, low = split(value)
    t_high, t_low = tables[flip, parity, 0], tables[flip, parity, 1]
    return dot(t_high, high) + (dot(t_high, low) + dot(t_low, high))


def table_right(tables, flip, parity, value):
    high, low = split(value)
    t_high, t_low = tables[flip, parity, 0], tables[flip, parity, 1]
    return dot(high, t_high) + (dot(low, t_high) + dot(high, t_low))


def rows_cat(a, b):
    return jnp.concatenate([a, b], axis=0)


def lanes_cat(a, b):
    return jnp.concatenate([a, b], axis=1)


def forward(tables, re, im):
    ra, rb, ia, ib = re[:HALF], re[HALF:], im[:HALF], im[HALF:]
    even = table_left(tables, 0, 0, rows_cat(ra + rb, ia + ib))
    odd = table_left(tables, 0, 1, rows_cat(ra - rb, ia - ib))
    real = rows_cat(even[:HALF], odd[:HALF])
    imag = rows_cat(even[HALF:], odd[HALF:])
    ra, rb, ia, ib = real[:, :HALF], real[:, HALF:], imag[:, :HALF], imag[:, HALF:]
    return (
        table_right(tables, 1, 0, lanes_cat(ra + rb, ia + ib)),
        table_right(tables, 1, 1, lanes_cat(ra - rb, ia - ib)),
    )


def inverse(tables, even, odd):
    even = table_right(tables, 0, 0, even)
    odd = table_right(tables, 0, 1, odd)
    real = lanes_cat(even[:, :HALF] + odd[:, :HALF], even[:, :HALF] - odd[:, :HALF])
    imag = lanes_cat(even[:, HALF:] + odd[:, HALF:], even[:, HALF:] - odd[:, HALF:])
    even = table_left(tables, 1, 0, rows_cat(real[:HALF], imag[:HALF]))
    odd = table_left(tables, 1, 1, rows_cat(real[HALF:], imag[HALF:]))
    return (
        rows_cat(even[:HALF] + odd[:HALF], even[:HALF] - odd[:HALF]),
        rows_cat(even[HALF:] + odd[HALF:], even[HALF:] - odd[HALF:]),
    )


def masks(off_ref, iteration, slot):
    row = off_ref[iteration, slot, 0]
    col = off_ref[iteration, slot, 1]
    below = lax.broadcasted_iota(jnp.int32, (SIDE, SIDE), 0) < row
    right = lax.broadcasted_iota(jnp.int32, (SIDE, SIDE), 1) < col
    return below, right


def picked(below, right, own, rgt, low, dia, plane):
    upper = jnp.where(right, rgt[plane], own[plane])
    lower = jnp.where(right, dia[plane], low[plane])
    return jnp.where(below, lower, upper)


def placed(below, right, value, plane, stay, side, diag):
    zero = jnp.zeros_like(value)
    left_part = jnp.where(right, zero, value)
    right_part = jnp.where(right, value, zero)
    stay[0, plane] += jnp.where(below, zero, left_part)
    stay[1, plane] += jnp.where(below, left_part, zero)
    side[plane] += jnp.where(below, zero, right_part)
    diag[plane] += jnp.where(below, right_part, zero)


def prepare_kernel(off_ref, probe_ref, cos_ref, sin_ref, amp_ref, perm_ref,
                   rolled_ref, prop_ref, ampl_ref, twice):
    def reorder(src):
        rest = src[...]
        total = None
        for _ in range(3):
            part = rest.astype(jnp.bfloat16)
            rest = rest - part.astype(jnp.float32)
            part = dot(dot(perm_ref[0], part).astype(jnp.bfloat16), perm_ref[1])
            total = part if total is None else total + part
        return total

    def put(dst, value):
        dst[0] = value[:, :HALF]
        dst[1] = value[:, HALF:]

    def tile_loop(index, carry):
        it, slot = index // SLOTS, index % SLOTS
        row = off_ref[it, slot, 0]
        col = off_ref[it, slot, 1]
        for plane in range(2):
            start = pl.multiple_of(SIDE - 8 - row // 8 * 8, 8)
            turned = pltpu.roll(twice[plane, pl.ds(start, SIDE + 8), :], row % 8, 0)
            rolled_ref[it, slot, plane] = pltpu.roll(turned[8:], col, 1)
        put(ampl_ref.at[it, slot], reorder(amp_ref.at[it, slot]))
        return carry

    for plane in range(2):
        twice[plane, :SIDE] = probe_ref[plane]
        twice[plane, SIDE:] = probe_ref[plane]
    put(prop_ref.at[0], reorder(cos_ref))
    put(prop_ref.at[1], reorder(sin_ref))
    lax.fori_loop(0, ITERS * SLOTS, tile_loop, 0)


def first_kernel(iteration, off_ref, cnt_ref, rolled, prop, tables, *refs):
    *tiles, mid_ref = refs
    own, rgt, low, dia = tiles

    def body(slot, carry):
        below, right = masks(off_ref, iteration, slot)
        one_re = picked(below, right, own, rgt, low, dia, 0)
        one_im = picked(below, right, own, rgt, low, dia, 1)
        p_re, p_im = rolled[iteration, slot, 0], rolled[iteration, slot, 1]
        spec = forward(tables, p_re * one_re - p_im * one_im, p_re * one_im + p_im * one_re)
        moved = []
        for q in range(2):
            re, im = spec[q][:, :HALF], spec[q][:, HALF:]
            h_re, h_im = prop[0, q], prop[1, q]
            moved.append(lanes_cat(re * h_re - im * h_im, re * h_im + im * h_re))
        mid_ref[slot, 0], mid_ref[slot, 1] = inverse(tables, *moved)
        return carry

    lax.fori_loop(0, cnt_ref[iteration], body, 0)


def second_kernel(iteration, off_ref, cnt_ref, mid_ref, ampl, tables, *refs):
    own, rgt, low, dia, stay, *moves, carry_ref = refs
    side, diag = moves if len(moves) == 2 else (moves[0].at[0], moves[0].at[1])
    stay[...] = jnp.zeros_like(stay)
    side[...] = jnp.zeros_like(side)
    diag[...] = jnp.zeros_like(diag)

    def body(slot, carry):
        below, right = masks(off_ref, iteration, slot)
        two_re = picked(below, right, own, rgt, low, dia, 0)
        two_im = picked(below, right, own, rgt, low, dia, 1)
        m_re, m_im = mid_ref[slot, 0], mid_ref[slot, 1]
        far = forward(tables, m_re * two_re - m_im * two_im, m_re * two_im + m_im * two_re)
        chi = []
        for q in range(2):
            re, im = far[q][:, :HALF], far[q][:, HALF:]
            factor = 1.0 - ampl[iteration, slot, q] * lax.rsqrt(re * re + im * im + soft_floor)
            chi.append(lanes_cat(re * factor, im * factor))
        b_re, b_im = inverse(tables, *chi)
        placed(below, right, m_re * b_re + m_im * b_im, 0, stay, side, diag)
        placed(below, right, m_re * b_im - m_im * b_re, 1, stay, side, diag)
        carry_ref[slot, 0] = two_re * b_re + two_im * b_im
        carry_ref[slot, 1] = two_re * b_im - two_im * b_re
        return carry

    lax.fori_loop(0, cnt_ref[iteration], body, 0)


def third_kernel(iteration, off_ref, cnt_ref, carry_ref, rolled, prop, tables, stay, *moves):
    side, diag = moves if len(moves) == 2 else (moves[0].at[0], moves[0].at[1])
    stay[...] = jnp.zeros_like(stay)
    side[...] = jnp.zeros_like(side)
    diag[...] = jnp.zeros_like(diag)

    def body(slot, carry):
        below, right = masks(off_ref, iteration, slot)
        spec = forward(tables, carry_ref[slot, 0], carry_ref[slot, 1])
        turned = []
        for q in range(2):
            re, im = spec[q][:, :HALF], spec[q][:, HALF:]
            h_re, h_im = prop[0, q], prop[1, q]
            turned.append(lanes_cat(re * h_re + im * h_im, im * h_re - re * h_im))
        e_re, e_im = inverse(tables, *turned)
        p_re, p_im = rolled[iteration, slot, 0], rolled[iteration, slot, 1]
        placed(below, right, p_re * e_re + p_im * e_im, 0, stay, side, diag)
        placed(below, right, p_re * e_im - p_im * e_re, 1, stay, side, diag)
        return carry

    lax.fori_loop(0, cnt_ref[iteration], body, 0)


def sums_kernel(first, stay, side, diag, above, below):
    for plane in range(2):
        zero = jnp.zeros((SIDE, SIDE), jnp.float32)
        extra = diag[plane]
        above[plane] = stay[0, plane] + side[plane] + jnp.where(first[0] > 0, extra, zero)
        below[plane] = stay[1, plane] + jnp.where(first[0] > 0, zero, extra)


def fall_kernel(stay, came, above, *below):
    above[...] = stay[0] + came[0]
    if len(below) == 1:
        below[0][...] = stay[1] + came[1]
    else:
        for plane in range(2):
            below[plane][...] = stay[1, plane] + came[1, plane]


def update_kernel(first, above, below, from_above, from_below, old, old_low, own, low, send):
    for plane in range(2):
        one = old[plane] - step_size * (above[plane] + from_above[plane])
        two = old_low[plane] - step_size * (from_below[plane] + below[plane])
        own[plane] = one
        low[plane] = two
        send[plane] = jnp.where(first[0] > 0, one, two)


def last_kernel(one, two, above1, above2, near2, far2, fallen1, out):
    out[0] = one[...] - step_size * (above1[...] + fallen1[...])
    out[1, 0] = two[0] - step_size * (above2[0] + near2[...])
    out[1, 1] = two[1] - step_size * (above2[1] + far2[...])


SMEM = pl.BlockSpec(memory_space=pltpu.SMEM)
VMEM = pl.BlockSpec(memory_space=pltpu.VMEM)
LIMIT = 12 * 1024 * 1024


def f32(*shape):
    return jax.ShapeDtypeStruct(shape, jnp.float32)


def call(body, scalars, arrays, outs, scratch=(), flops=4 * 10**9):
    args = [*scalars, *arrays]
    return pl.pallas_call(
        body,
        out_shape=outs,
        in_specs=[SMEM] * len(scalars) + [VMEM] * len(arrays),
        out_specs=[VMEM] * len(outs),
        scratch_shapes=scratch,
        compiler_params=pltpu.CompilerParams(vmem_limit_bytes=LIMIT),
        cost_estimate=pl.CostEstimate(flops=flops, bytes_accessed=8 * 2**20, transcendentals=0),
    )(*args)


def shards(object_tiles, probe_field, prop_angle, scan_offsets, probe_counts, amplitudes):
    tables = jnp.asarray(dft_tables())
    lane = np.arange(SIDE)
    source = np.concatenate([lane[0::2], lane[1::2]])
    perm = np.zeros((SIDE, SIDE), np.float32)
    perm[source, lane] = 1.0
    perm = jnp.asarray(np.stack([perm.T, perm]).astype(jnp.bfloat16))
    offsets = scan_offsets.reshape(ITERS, SLOTS, 2)
    counts = probe_counts.reshape(ITERS)
    measured = amplitudes.reshape(ITERS, SLOTS, SIDE, SIDE)

    sizes = lax.axis_size("ty"), lax.axis_size("tx")
    sizes = lax.axis_size("ty"), lax.axis_size("tx")
    column = lax.axis_index("tx") % 4
    first = (column == 0).astype(jnp.int32).reshape(1)
    own = [object_tiles[0], object_tiles[1]]
    low0 = shifted(own[0], "ty", -1)
    far = around(object_tiles[1, 1], -1, sizes)
    rgt = [shifted(own[s], "tx", -1) for s in (0, 1)]
    near = shifted(object_tiles[1, 0], "ty", -1)
    low = [low0, jnp.stack([near, far])]
    dia = [shifted(low[s], "tx", -1) for s in (0, 1)]

    rolled, prop, ampl = call(
        prepare_kernel, [offsets],
        [probe_field, jnp.cos(prop_angle), jnp.sin(prop_angle), measured, perm],
        [f32(ITERS, SLOTS, 2, SIDE, SIDE), f32(2, 2, SIDE, HALF), f32(ITERS, SLOTS, 2, SIDE, HALF)],
        [pltpu.VMEM((2, 2 * SIDE, SIDE), jnp.float32)],
    )
    pair, tile = f32(2, 2, SIDE, SIDE), f32(2, SIDE, SIDE)

    tiles = [[own[s], rgt[s], low[s], dia[s]] for s in (0, 1)]

    for iteration in range(ITERS):
        def bind(kernel, iteration=iteration):
            return lambda *refs: kernel(iteration, *refs)

        scalars = [offsets, counts]
        (mid,) = call(bind(first_kernel), scalars, [rolled, prop, tables, *tiles[0]], [pair])
        last = iteration == ITERS - 1
        moves = [pair] if last else [tile, tile]
        stay2, *moves2, carry = call(bind(second_kernel), scalars,
                                     [mid, ampl, tables, *tiles[1]], [pair, *moves, pair])
        stay1, *moves1 = call(bind(third_kernel), scalars,
                              [carry, rolled, prop, tables], [pair, *moves])
        stay = [stay1, stay2]
        if last:
            came = [None, None]
            for s in (1, 0):
                came[s] = shifted([moves1, moves2][s][0], "tx", 1)
            above2, near, far = call(fall_kernel, [], [stay[1], came[1]],
                                     [tile, f32(SIDE, SIDE), f32(SIDE, SIDE)], flops=10**6)
            above1, fallen = call(fall_kernel, [], [stay[0], came[0]], [tile, tile], flops=10**6)
            far = around(far, 1, sizes)
            near = shifted(near, "ty", 1)
            fallen = shifted(fallen, "ty", 1)
            (out,) = call(last_kernel, [], [tiles[0][0], tiles[1][0], above1, above2, near, far, fallen],
                          [pair], flops=10**6)
            return out
        side, diag = [moves1[0], moves2[0]], [moves1[1], moves2[1]]
        for s in (1, 0):
            diag[s] = moved(diag[s], diagonal_on, sizes)
        above, below = [None, None], [None, None]
        for s in (1, 0):
            side[s] = shifted(side[s], "tx", 1)
            above[s], below[s] = call(sums_kernel, [first], [stay[s], side[s], diag[s]],
                                      [tile, tile], flops=10**6)
        for s in (1, 0):
            fallen = shifted(below[s], "ty", 1)
            risen = shifted(above[s], "ty", -1)
            own, low, send = call(update_kernel, [first],
                                  [above[s], below[s], fallen, risen, tiles[s][0], tiles[s][2]],
                                  [tile] * 3, flops=10**6)
            tiles[s] = [own, shifted(own, "tx", -1), low,
                        moved(send, diagonal_back, sizes)]


def solution(mesh):
    in_specs = (
        P(None, None, "ty", "tx"),
        P(),
        P(),
        P(None, "ty", "tx", None, None),
        P(None, "ty", "tx"),
        P(None, "ty", "tx", None, None, None),
    )
    out_specs = P(None, None, "ty", "tx")

    return jax.shard_map(shards, mesh=mesh, in_specs=in_specs, out_specs=out_specs, check_vma=False)
```

```python
import numpy as np

import jax
import jax.numpy as jnp
from jax import lax
from jax.experimental import pallas as pl
from jax.experimental.pallas import tpu as pltpu
from jax.sharding import PartitionSpec as P


ITERS = 2
SLOTS = 2
SIDE = 256
HALF = SIDE // 2

soft_floor = 0.01
step_size = 0.25


def dft_tables():
    k = np.arange(HALF)
    stack = []
    for parity in (0, 1):
        angle = 2.0 * np.pi * ((2 * k[:, None] + parity) * k[None, :] % SIDE) / SIDE
        cos, sin = np.cos(angle) / 16.0, np.sin(angle) / 16.0
        stack.append(np.block([[cos, sin], [-sin, cos]]))
    both = np.stack([np.stack(stack), np.stack([t.T for t in stack])])
    high = both.astype(jnp.bfloat16)
    low = (both - high.astype(np.float64)).astype(jnp.bfloat16)
    return np.stack([high, low], axis=2)


def shifted(value, axis, steps):
    count = lax.axis_size(axis)
    first, last = (max(0, -steps), min(count, count - steps))
    return lax.ppermute(value, axis, [(source, source + steps) for source in range(first, last)])


def moved(value, target, sizes):
    rows, cols = sizes
    pairs = []
    for row in range(rows):
        for col in range(cols):
            new_row, new_col = target(row, col)
            if 0 <= new_row < rows and 0 <= new_col < cols:
                pairs.append((row * cols + col, new_row * cols + new_col))
    return lax.ppermute(value, ("ty", "tx"), pairs)


NOWHERE = (-1, -1)


def diagonal_back(row, col):
    return (row - 1, col - 1) if col % 4 == 0 else (row, col - 1)


def diagonal_on(row, col):
    return (row + 1, col + 1) if col % 4 == 3 else (row, col + 1)


def around(value, steps, sizes):
    rows, cols = sizes

    def relay(row, col):
        z = (2 * (row % 4) + col // 2 % 2 - 3 * steps) % 8
        return row // 4 * 4 + z // 2, col // 4 * 4 + z % 2 * 2 + col % 2

    spots = [(r, c) for r in range(rows) for c in range(cols) if 0 <= r + steps < rows]
    ends = {relay(*spot): (spot[0] + steps, spot[1]) for spot in spots}
    value = moved(value, lambda r, c: relay(r, c) if (r, c) in spots else NOWHERE, sizes)
    return moved(value, lambda r, c: ends.get((r, c), NOWHERE), sizes)


def split(value):
    high = value.astype(jnp.bfloat16)
    return high, (value - high.astype(jnp.float32)).astype(jnp.bfloat16)


def dot(left, right):
    return jnp.dot(left, right, preferred_element_type=jnp.float32)


def table_left(tables, flip, parity, value):
    high, low = split(value)
    t_high, t_low = tables[flip, parity, 0], tables[flip, parity, 1]
    return dot(t_high, high) + (dot(t_high, low) + dot(t_low, high))


def table_right(tables, flip, parity, value):
    high, low = split(value)
    t_high, t_low = tables[flip, parity, 0], tables[flip, parity, 1]
    return dot(high, t_high) + (dot(low, t_high) + dot(high, t_low))


def rows_cat(a, b):
    return jnp.concatenate([a, b], axis=0)


def lanes_cat(a, b):
    return jnp.concatenate([a, b], axis=1)


def forward(tables, re, im):
    ra, rb, ia, ib = re[:HALF], re[HALF:], im[:HALF], im[HALF:]
    even = table_left(tables, 0, 0, rows_cat(ra + rb, ia + ib))
    odd = table_left(tables, 0, 1, rows_cat(ra - rb, ia - ib))
    real = rows_cat(even[:HALF], odd[:HALF])
    imag = rows_cat(even[HALF:], odd[HALF:])
    ra, rb, ia, ib = real[:, :HALF], real[:, HALF:], imag[:, :HALF], imag[:, HALF:]
    return (
        table_right(tables, 1, 0, lanes_cat(ra + rb, ia + ib)),
        table_right(tables, 1, 1, lanes_cat(ra - rb, ia - ib)),
    )


def inverse(tables, even, odd):
    even = table_right(tables, 0, 0, even)
    odd = table_right(tables, 0, 1, odd)
    real = lanes_cat(even[:, :HALF] + odd[:, :HALF], even[:, :HALF] - odd[:, :HALF])
    imag = lanes_cat(even[:, HALF:] + odd[:, HALF:], even[:, HALF:] - odd[:, HALF:])
    even = table_left(tables, 1, 0, rows_cat(real[:HALF], imag[:HALF]))
    odd = table_left(tables, 1, 1, rows_cat(real[HALF:], imag[HALF:]))
    return (
        rows_cat(even[:HALF] + odd[:HALF], even[:HALF] - odd[:HALF]),
        rows_cat(even[HALF:] + odd[HALF:], even[HALF:] - odd[HALF:]),
    )


def masks(off_ref, iteration, slot):
    row = off_ref[iteration, slot, 0]
    col = off_ref[iteration, slot, 1]
    below = lax.broadcasted_iota(jnp.int32, (SIDE, SIDE), 0) < row
    right = lax.broadcasted_iota(jnp.int32, (SIDE, SIDE), 1) < col
    return below, right


def picked(below, right, own, rgt, low, dia, plane):
    upper = jnp.where(right, rgt[plane], own[plane])
    lower = jnp.where(right, dia[plane], low[plane])
    return jnp.where(below, lower, upper)


def placed(below, right, value, plane, stay, side, diag):
    zero = jnp.zeros_like(value)
    left_part = jnp.where(right, zero, value)
    right_part = jnp.where(right, value, zero)
    stay[0, plane] += jnp.where(below, zero, left_part)
    stay[1, plane] += jnp.where(below, left_part, zero)
    side[plane] += jnp.where(below, zero, right_part)
    diag[plane] += jnp.where(below, right_part, zero)


def prepare_kernel(off_ref, probe_ref, angle_ref, amp_ref, perm_ref,
                   rolled_ref, prop_ref, ampl_ref, twice):
    def reorder(src):
        rest = src
        total = None
        for _ in range(3):
            part = rest.astype(jnp.bfloat16)
            rest = rest - part.astype(jnp.float32)
            part = dot(dot(perm_ref[0], part).astype(jnp.bfloat16), perm_ref[1])
            total = part if total is None else total + part
        return total

    def put(dst, value):
        dst[0] = value[:, :HALF]
        dst[1] = value[:, HALF:]

    def tile_loop(index, carry):
        it, slot = index // SLOTS, index % SLOTS
        row = off_ref[it, slot, 0]
        col = off_ref[it, slot, 1]
        for plane in range(2):
            start = pl.multiple_of(SIDE - 8 - row // 8 * 8, 8)
            turned = pltpu.roll(twice[plane, pl.ds(start, SIDE + 8), :], row % 8, 0)
            rolled_ref[it, slot, plane] = pltpu.roll(turned[8:], col, 1)
        put(ampl_ref.at[it, slot], reorder(amp_ref[it, slot]))
        return carry

    for plane in range(2):
        twice[plane, :SIDE] = probe_ref[plane]
        twice[plane, SIDE:] = probe_ref[plane]
    put(prop_ref.at[0], reorder(jnp.cos(angle_ref[...])))
    put(prop_ref.at[1], reorder(jnp.sin(angle_ref[...])))
    lax.fori_loop(0, ITERS * SLOTS, tile_loop, 0)


def first_kernel(iteration, off_ref, cnt_ref, rolled, prop, tables, *refs):
    *tiles, mid_ref = refs
    own, rgt, low, dia = tiles

    def body(slot, carry):
        below, right = masks(off_ref, iteration, slot)
        one_re = picked(below, right, own, rgt, low, dia, 0)
        one_im = picked(below, right, own, rgt, low, dia, 1)
        p_re, p_im = rolled[iteration, slot, 0], rolled[iteration, slot, 1]
        spec = forward(tables, p_re * one_re - p_im * one_im, p_re * one_im + p_im * one_re)
        moved = []
        for q in range(2):
            re, im = spec[q][:, :HALF], spec[q][:, HALF:]
            h_re, h_im = prop[0, q], prop[1, q]
            moved.append(lanes_cat(re * h_re - im * h_im, re * h_im + im * h_re))
        mid_ref[slot, 0], mid_ref[slot, 1] = inverse(tables, *moved)
        return carry

    lax.fori_loop(0, cnt_ref[iteration], body, 0)


def second_kernel(iteration, off_ref, cnt_ref, mid_ref, ampl, tables, *refs):
    own, rgt, low, dia, stay, *moves, carry_ref = refs
    side, diag = moves if len(moves) == 2 else (moves[0].at[0], moves[0].at[1])
    stay[...] = jnp.zeros_like(stay)
    side[...] = jnp.zeros_like(side)
    diag[...] = jnp.zeros_like(diag)

    def body(slot, carry):
        below, right = masks(off_ref, iteration, slot)
        two_re = picked(below, right, own, rgt, low, dia, 0)
        two_im = picked(below, right, own, rgt, low, dia, 1)
        m_re, m_im = mid_ref[slot, 0], mid_ref[slot, 1]
        far = forward(tables, m_re * two_re - m_im * two_im, m_re * two_im + m_im * two_re)
        chi = []
        for q in range(2):
            re, im = far[q][:, :HALF], far[q][:, HALF:]
            factor = 1.0 - ampl[iteration, slot, q] * lax.rsqrt(re * re + im * im + soft_floor)
            chi.append(lanes_cat(re * factor, im * factor))
        b_re, b_im = inverse(tables, *chi)
        placed(below, right, m_re * b_re + m_im * b_im, 0, stay, side, diag)
        placed(below, right, m_re * b_im - m_im * b_re, 1, stay, side, diag)
        carry_ref[slot, 0] = two_re * b_re + two_im * b_im
        carry_ref[slot, 1] = two_re * b_im - two_im * b_re
        return carry

    lax.fori_loop(0, cnt_ref[iteration], body, 0)


def third_kernel(iteration, off_ref, cnt_ref, carry_ref, rolled, prop, tables, stay, *moves):
    side, diag = moves if len(moves) == 2 else (moves[0].at[0], moves[0].at[1])
    stay[...] = jnp.zeros_like(stay)
    side[...] = jnp.zeros_like(side)
    diag[...] = jnp.zeros_like(diag)

    def body(slot, carry):
        below, right = masks(off_ref, iteration, slot)
        spec = forward(tables, carry_ref[slot, 0], carry_ref[slot, 1])
        turned = []
        for q in range(2):
            re, im = spec[q][:, :HALF], spec[q][:, HALF:]
            h_re, h_im = prop[0, q], prop[1, q]
            turned.append(lanes_cat(re * h_re + im * h_im, im * h_re - re * h_im))
        e_re, e_im = inverse(tables, *turned)
        p_re, p_im = rolled[iteration, slot, 0], rolled[iteration, slot, 1]
        placed(below, right, p_re * e_re + p_im * e_im, 0, stay, side, diag)
        placed(below, right, p_re * e_im - p_im * e_re, 1, stay, side, diag)
        return carry

    lax.fori_loop(0, cnt_ref[iteration], body, 0)


def leading():
    return lax.rem(lax.axis_index("tx"), 4) == 0


def join_kernel(near, far, both):
    both[0] = near[...]
    both[1] = far[...]


def sums_kernel(stay, side, diag, above, below):
    for plane in range(2):
        zero = jnp.zeros((SIDE, SIDE), jnp.float32)
        extra = diag[plane]
        above[plane] = stay[0, plane] + side[plane] + jnp.where(leading(), extra, zero)
        below[plane] = stay[1, plane] + jnp.where(leading(), zero, extra)


def fall_kernel(stay, came, above, *below):
    above[...] = stay[0] + came[0]
    if len(below) == 1:
        below[0][...] = stay[1] + came[1]
    else:
        for plane in range(2):
            below[plane][...] = stay[1, plane] + came[1, plane]


def update_kernel(above, below, from_above, from_below, old, old_low, own, low, send):
    for plane in range(2):
        one = old[plane] - step_size * (above[plane] + from_above[plane])
        two = old_low[plane] - step_size * (from_below[plane] + below[plane])
        own[plane] = one
        low[plane] = two
        send[plane] = jnp.where(leading(), one, two)


def last_kernel(one, two, above1, above2, near2, far2, fallen1, out):
    out[0] = one[...] - step_size * (above1[...] + fallen1[...])
    out[1, 0] = two[0] - step_size * (above2[0] + near2[...])
    out[1, 1] = two[1] - step_size * (above2[1] + far2[...])


SMEM = pl.BlockSpec(memory_space=pltpu.SMEM)
VMEM = pl.BlockSpec(memory_space=pltpu.VMEM)
LIMIT = 12 * 1024 * 1024


def f32(*shape):
    return jax.ShapeDtypeStruct(shape, jnp.float32)


def call(body, scalars, arrays, outs, scratch=(), flops=4 * 10**9):
    args = [*scalars, *arrays]
    return pl.pallas_call(
        body,
        out_shape=outs,
        in_specs=[SMEM] * len(scalars) + [VMEM] * len(arrays),
        out_specs=[VMEM] * len(outs),
        scratch_shapes=scratch,
        compiler_params=pltpu.CompilerParams(vmem_limit_bytes=LIMIT),
        cost_estimate=pl.CostEstimate(flops=flops, bytes_accessed=8 * 2**20, transcendentals=0),
    )(*args)


def shards(object_tiles, probe_field, prop_angle, scan_offsets, probe_counts, amplitudes):
    tables = jnp.asarray(dft_tables())
    lane = np.arange(SIDE)
    source = np.concatenate([lane[0::2], lane[1::2]])
    perm = np.zeros((SIDE, SIDE), np.float32)
    perm[source, lane] = 1.0
    perm = jnp.asarray(np.stack([perm.T, perm]).astype(jnp.bfloat16))
    offsets = scan_offsets.reshape(ITERS, SLOTS, 2)
    counts = probe_counts.reshape(ITERS)
    measured = amplitudes.reshape(ITERS, SLOTS, SIDE, SIDE)

    sizes = lax.axis_size("ty"), lax.axis_size("tx")
    sizes = lax.axis_size("ty"), lax.axis_size("tx")
    own = [object_tiles[0], object_tiles[1]]
    low0 = shifted(own[0], "ty", -1)
    far = around(object_tiles[1, 1], -1, sizes)
    rgt = [shifted(own[s], "tx", -1) for s in (0, 1)]
    near = shifted(object_tiles[1, 0], "ty", -1)
    (low1,) = call(join_kernel, [], [near, far], [f32(2, SIDE, SIDE)], flops=10**6)
    low = [low0, low1]
    dia = [shifted(low[s], "tx", -1) for s in (0, 1)]

    rolled, prop, ampl = call(
        prepare_kernel, [offsets],
        [probe_field, prop_angle, measured, perm],
        [f32(ITERS, SLOTS, 2, SIDE, SIDE), f32(2, 2, SIDE, HALF), f32(ITERS, SLOTS, 2, SIDE, HALF)],
        [pltpu.VMEM((2, 2 * SIDE, SIDE), jnp.float32)],
    )
    pair, tile = f32(2, 2, SIDE, SIDE), f32(2, SIDE, SIDE)

    tiles = [[own[s], rgt[s], low[s], dia[s]] for s in (0, 1)]

    for iteration in range(ITERS):
        def bind(kernel, iteration=iteration):
            return lambda *refs: kernel(iteration, *refs)

        scalars = [offsets, counts]
        (mid,) = call(bind(first_kernel), scalars, [rolled, prop, tables, *tiles[0]], [pair])
        last = iteration == ITERS - 1
        moves = [pair] if last else [tile, tile]
        stay2, *moves2, carry = call(bind(second_kernel), scalars,
                                     [mid, ampl, tables, *tiles[1]], [pair, *moves, pair])
        stay1, *moves1 = call(bind(third_kernel), scalars,
                              [carry, rolled, prop, tables], [pair, *moves])
        stay = [stay1, stay2]
        if last:
            came = [None, None]
            for s in (1, 0):
                came[s] = shifted([moves1, moves2][s][0], "tx", 1)
            above2, near, far = call(fall_kernel, [], [stay[1], came[1]],
                                     [tile, f32(SIDE, SIDE), f32(SIDE, SIDE)], flops=10**6)
            above1, fallen = call(fall_kernel, [], [stay[0], came[0]], [tile, tile], flops=10**6)
            far = around(far, 1, sizes)
            near = shifted(near, "ty", 1)
            fallen = shifted(fallen, "ty", 1)
            (out,) = call(last_kernel, [], [tiles[0][0], tiles[1][0], above1, above2, near, far, fallen],
                          [pair], flops=10**6)
            return out
        side, diag = [moves1[0], moves2[0]], [moves1[1], moves2[1]]
        for s in (1, 0):
            diag[s] = moved(diag[s], diagonal_on, sizes)
        above, below = [None, None], [None, None]
        for s in (1, 0):
            side[s] = shifted(side[s], "tx", 1)
            above[s], below[s] = call(sums_kernel, [], [stay[s], side[s], diag[s]],
                                      [tile, tile], flops=10**6)
        for s in (1, 0):
            fallen = shifted(below[s], "ty", 1)
            risen = shifted(above[s], "ty", -1)
            own, low, send = call(update_kernel, [],
                                  [above[s], below[s], fallen, risen, tiles[s][0], tiles[s][2]],
                                  [tile] * 3, flops=10**6)
            tiles[s] = [own, shifted(own, "tx", -1), low,
                        moved(send, diagonal_back, sizes)]


def solution(mesh):
    in_specs = (
        P(None, None, "ty", "tx"),
        P(),
        P(),
        P(None, "ty", "tx", None, None),
        P(None, "ty", "tx"),
        P(None, "ty", "tx", None, None, None),
    )
    out_specs = P(None, None, "ty", "tx")

    return jax.shard_map(shards, mesh=mesh, in_specs=in_specs, out_specs=out_specs, check_vma=False)
```

```python
import numpy as np

import jax
import jax.numpy as jnp
from jax import lax
from jax.experimental import pallas as pl
from jax.experimental.pallas import tpu as pltpu
from jax.sharding import PartitionSpec as P


ITERS = 2
SLOTS = 2
SIDE = 256
HALF = SIDE // 2

soft_floor = 0.01
step_size = 0.25


def dft_tables():
    k = np.arange(HALF)
    stack = []
    for parity in (0, 1):
        angle = 2.0 * np.pi * ((2 * k[:, None] + parity) * k[None, :] % SIDE) / SIDE
        cos, sin = np.cos(angle) / 16.0, np.sin(angle) / 16.0
        stack.append(np.block([[cos, sin], [-sin, cos]]))
    both = np.stack([np.stack(stack), np.stack([t.T for t in stack])])
    high = both.astype(jnp.bfloat16)
    low = (both - high.astype(np.float64)).astype(jnp.bfloat16)
    return np.stack([high, low], axis=2)


def shifted(value, axis, steps):
    count = lax.axis_size(axis)
    first, last = (max(0, -steps), min(count, count - steps))
    return lax.ppermute(value, axis, [(source, source + steps) for source in range(first, last)])


def moved(value, target, sizes):
    rows, cols = sizes
    pairs = []
    for row in range(rows):
        for col in range(cols):
            new_row, new_col = target(row, col)
            if 0 <= new_row < rows and 0 <= new_col < cols:
                pairs.append((row * cols + col, new_row * cols + new_col))
    return lax.ppermute(value, ("ty", "tx"), pairs)


NOWHERE = (-1, -1)


def diagonal_back(row, col):
    return (row - 1, col - 1) if col % 4 == 0 else (row, col - 1)


def diagonal_on(row, col):
    return (row + 1, col + 1) if col % 4 == 3 else (row, col + 1)


def around(value, steps, sizes):
    rows, cols = sizes

    def relay(row, col):
        z = (2 * (row % 4) + col // 2 % 2 - 3 * steps) % 8
        return row // 4 * 4 + z // 2, col // 4 * 4 + z % 2 * 2 + col % 2

    spots = [(r, c) for r in range(rows) for c in range(cols) if 0 <= r + steps < rows]
    ends = {relay(*spot): (spot[0] + steps, spot[1]) for spot in spots}
    value = moved(value, lambda r, c: relay(r, c) if (r, c) in spots else NOWHERE, sizes)
    return moved(value, lambda r, c: ends.get((r, c), NOWHERE), sizes)


def split(value):
    high = value.astype(jnp.bfloat16)
    return high, (value - high.astype(jnp.float32)).astype(jnp.bfloat16)


def dot(left, right):
    return jnp.dot(left, right, preferred_element_type=jnp.float32)


def table_left(tables, flip, parity, value):
    high, low = split(value)
    t_high, t_low = tables[flip, parity, 0], tables[flip, parity, 1]
    return dot(t_high, high) + (dot(t_high, low) + dot(t_low, high))


def table_right(tables, flip, parity, value):
    high, low = split(value)
    t_high, t_low = tables[flip, parity, 0], tables[flip, parity, 1]
    return dot(high, t_high) + (dot(low, t_high) + dot(high, t_low))


def rows_cat(a, b):
    return jnp.concatenate([a, b], axis=0)


def lanes_cat(a, b):
    return jnp.concatenate([a, b], axis=1)


def forward(tables, re, im):
    ra, rb, ia, ib = re[:HALF], re[HALF:], im[:HALF], im[HALF:]
    even = table_left(tables, 0, 0, rows_cat(ra + rb, ia + ib))
    odd = table_left(tables, 0, 1, rows_cat(ra - rb, ia - ib))
    real = rows_cat(even[:HALF], odd[:HALF])
    imag = rows_cat(even[HALF:], odd[HALF:])
    ra, rb, ia, ib = real[:, :HALF], real[:, HALF:], imag[:, :HALF], imag[:, HALF:]
    return (
        table_right(tables, 1, 0, lanes_cat(ra + rb, ia + ib)),
        table_right(tables, 1, 1, lanes_cat(ra - rb, ia - ib)),
    )


def inverse(tables, even, odd):
    even = table_right(tables, 0, 0, even)
    odd = table_right(tables, 0, 1, odd)
    real = lanes_cat(even[:, :HALF] + odd[:, :HALF], even[:, :HALF] - odd[:, :HALF])
    imag = lanes_cat(even[:, HALF:] + odd[:, HALF:], even[:, HALF:] - odd[:, HALF:])
    even = table_left(tables, 1, 0, rows_cat(real[:HALF], imag[:HALF]))
    odd = table_left(tables, 1, 1, rows_cat(real[HALF:], imag[HALF:]))
    return (
        rows_cat(even[:HALF] + odd[:HALF], even[:HALF] - odd[:HALF]),
        rows_cat(even[HALF:] + odd[HALF:], even[HALF:] - odd[HALF:]),
    )


def masks(off_ref, iteration, slot):
    row = off_ref[iteration, slot, 0]
    col = off_ref[iteration, slot, 1]
    below = lax.broadcasted_iota(jnp.int32, (SIDE, SIDE), 0) < row
    right = lax.broadcasted_iota(jnp.int32, (SIDE, SIDE), 1) < col
    return below, right


def picked(below, right, own, rgt, low, dia, plane):
    upper = jnp.where(right, rgt[plane], own[plane])
    lower = jnp.where(right, dia[plane], low[plane])
    return jnp.where(below, lower, upper)


def placed(below, right, value, plane, stay, side, diag):
    zero = jnp.zeros_like(value)
    left_part = jnp.where(right, zero, value)
    right_part = jnp.where(right, value, zero)
    stay[0, plane] += jnp.where(below, zero, left_part)
    stay[1, plane] += jnp.where(below, left_part, zero)
    side[plane] += jnp.where(below, zero, right_part)
    diag[plane] += jnp.where(below, right_part, zero)


def prepare_kernel(off_ref, probe_ref, angle_ref, amp_ref, perm_ref,
                   rolled_ref, prop_ref, ampl_ref, twice):
    def reorder(src):
        rest = src
        total = None
        for _ in range(3):
            part = rest.astype(jnp.bfloat16)
            rest = rest - part.astype(jnp.float32)
            part = dot(dot(perm_ref[0], part).astype(jnp.bfloat16), perm_ref[1])
            total = part if total is None else total + part
        return total

    def put(dst, value):
        dst[0] = value[:, :HALF]
        dst[1] = value[:, HALF:]

    def tile_loop(index, carry):
        it, slot = index // SLOTS, index % SLOTS
        row = off_ref[it, slot, 0]
        col = off_ref[it, slot, 1]
        for plane in range(2):
            start = pl.multiple_of(SIDE - 8 - row // 8 * 8, 8)
            turned = pltpu.roll(twice[plane, pl.ds(start, SIDE + 8), :], row % 8, 0)
            rolled_ref[it, slot, plane] = pltpu.roll(turned[8:], col, 1)
        put(ampl_ref.at[it, slot], reorder(amp_ref[it, slot]))
        return carry

    for plane in range(2):
        twice[plane, :SIDE] = probe_ref[plane]
        twice[plane, SIDE:] = probe_ref[plane]
    put(prop_ref.at[0], reorder(jnp.cos(angle_ref[...])))
    put(prop_ref.at[1], reorder(jnp.sin(angle_ref[...])))
    lax.fori_loop(0, ITERS * SLOTS, tile_loop, 0)


def first_kernel(iteration, off_ref, cnt_ref, rolled, prop, tables, *refs):
    *tiles, mid_ref = refs
    own, rgt, low, dia = tiles

    def body(slot, carry):
        below, right = masks(off_ref, iteration, slot)
        one_re = picked(below, right, own, rgt, low, dia, 0)
        one_im = picked(below, right, own, rgt, low, dia, 1)
        p_re, p_im = rolled[iteration, slot, 0], rolled[iteration, slot, 1]
        spec = forward(tables, p_re * one_re - p_im * one_im, p_re * one_im + p_im * one_re)
        moved = []
        for q in range(2):
            re, im = spec[q][:, :HALF], spec[q][:, HALF:]
            h_re, h_im = prop[0, q], prop[1, q]
            moved.append(lanes_cat(re * h_re - im * h_im, re * h_im + im * h_re))
        mid_ref[slot, 0], mid_ref[slot, 1] = inverse(tables, *moved)
        return carry

    lax.fori_loop(0, cnt_ref[iteration], body, 0)


def second_kernel(iteration, off_ref, cnt_ref, mid_ref, ampl, tables, *refs):
    own, rgt, low, dia, stay, *moves, carry_ref = refs
    side, diag = moves if len(moves) == 2 else (moves[0].at[0], moves[0].at[1])
    stay[...] = jnp.zeros_like(stay)
    side[...] = jnp.zeros_like(side)
    diag[...] = jnp.zeros_like(diag)

    def body(slot, carry):
        below, right = masks(off_ref, iteration, slot)
        two_re = picked(below, right, own, rgt, low, dia, 0)
        two_im = picked(below, right, own, rgt, low, dia, 1)
        m_re, m_im = mid_ref[slot, 0], mid_ref[slot, 1]
        far = forward(tables, m_re * two_re - m_im * two_im, m_re * two_im + m_im * two_re)
        chi = []
        for q in range(2):
            re, im = far[q][:, :HALF], far[q][:, HALF:]
            factor = 1.0 - ampl[iteration, slot, q] * lax.rsqrt(re * re + im * im + soft_floor)
            chi.append(lanes_cat(re * factor, im * factor))
        b_re, b_im = inverse(tables, *chi)
        placed(below, right, m_re * b_re + m_im * b_im, 0, stay, side, diag)
        placed(below, right, m_re * b_im - m_im * b_re, 1, stay, side, diag)
        carry_ref[slot, 0] = two_re * b_re + two_im * b_im
        carry_ref[slot, 1] = two_re * b_im - two_im * b_re
        return carry

    lax.fori_loop(0, cnt_ref[iteration], body, 0)


def third_kernel(iteration, off_ref, cnt_ref, carry_ref, rolled, prop, tables, stay, *moves):
    side, diag = moves if len(moves) == 2 else (moves[0].at[0], moves[0].at[1])
    stay[...] = jnp.zeros_like(stay)
    side[...] = jnp.zeros_like(side)
    diag[...] = jnp.zeros_like(diag)

    def body(slot, carry):
        below, right = masks(off_ref, iteration, slot)
        spec = forward(tables, carry_ref[slot, 0], carry_ref[slot, 1])
        turned = []
        for q in range(2):
            re, im = spec[q][:, :HALF], spec[q][:, HALF:]
            h_re, h_im = prop[0, q], prop[1, q]
            turned.append(lanes_cat(re * h_re + im * h_im, im * h_re - re * h_im))
        e_re, e_im = inverse(tables, *turned)
        p_re, p_im = rolled[iteration, slot, 0], rolled[iteration, slot, 1]
        placed(below, right, p_re * e_re + p_im * e_im, 0, stay, side, diag)
        placed(below, right, p_re * e_im - p_im * e_re, 1, stay, side, diag)
        return carry

    lax.fori_loop(0, cnt_ref[iteration], body, 0)


def leading():
    return lax.rem(lax.axis_index("tx"), 4) == 0


def join_kernel(near, far, own, both, send):
    for plane, part in enumerate((near, far)):
        both[plane] = part[...]
        send[plane] = jnp.where(leading(), own[plane], part[...])


def choose_kernel(own, low, send):
    for plane in range(2):
        send[plane] = jnp.where(leading(), own[plane], low[plane])


def sums_kernel(stay, side, diag, above, below):
    for plane in range(2):
        zero = jnp.zeros((SIDE, SIDE), jnp.float32)
        extra = diag[plane]
        above[plane] = stay[0, plane] + side[plane] + jnp.where(leading(), extra, zero)
        below[plane] = stay[1, plane] + jnp.where(leading(), zero, extra)


def fall_kernel(stay, came, above, *below):
    above[...] = stay[0] + came[0]
    if len(below) == 1:
        below[0][...] = stay[1] + came[1]
    else:
        for plane in range(2):
            below[plane][...] = stay[1, plane] + came[1, plane]


def update_kernel(above, below, from_above, from_below, old, old_low, own, low, send):
    for plane in range(2):
        one = old[plane] - step_size * (above[plane] + from_above[plane])
        two = old_low[plane] - step_size * (from_below[plane] + below[plane])
        own[plane] = one
        low[plane] = two
        send[plane] = jnp.where(leading(), one, two)


def last_kernel(one, two, above1, above2, near2, far2, fallen1, out):
    out[0] = one[...] - step_size * (above1[...] + fallen1[...])
    out[1, 0] = two[0] - step_size * (above2[0] + near2[...])
    out[1, 1] = two[1] - step_size * (above2[1] + far2[...])


SMEM = pl.BlockSpec(memory_space=pltpu.SMEM)
VMEM = pl.BlockSpec(memory_space=pltpu.VMEM)
LIMIT = 12 * 1024 * 1024


def f32(*shape):
    return jax.ShapeDtypeStruct(shape, jnp.float32)


def call(body, scalars, arrays, outs, scratch=(), flops=4 * 10**9):
    args = [*scalars, *arrays]
    return pl.pallas_call(
        body,
        out_shape=outs,
        in_specs=[SMEM] * len(scalars) + [VMEM] * len(arrays),
        out_specs=[VMEM] * len(outs),
        scratch_shapes=scratch,
        compiler_params=pltpu.CompilerParams(vmem_limit_bytes=LIMIT),
        cost_estimate=pl.CostEstimate(flops=flops, bytes_accessed=8 * 2**20, transcendentals=0),
    )(*args)


def shards(object_tiles, probe_field, prop_angle, scan_offsets, probe_counts, amplitudes):
    tables = jnp.asarray(dft_tables())
    lane = np.arange(SIDE)
    source = np.concatenate([lane[0::2], lane[1::2]])
    perm = np.zeros((SIDE, SIDE), np.float32)
    perm[source, lane] = 1.0
    perm = jnp.asarray(np.stack([perm.T, perm]).astype(jnp.bfloat16))
    offsets = scan_offsets.reshape(ITERS, SLOTS, 2)
    counts = probe_counts.reshape(ITERS)
    measured = amplitudes.reshape(ITERS, SLOTS, SIDE, SIDE)

    sizes = lax.axis_size("ty"), lax.axis_size("tx")
    sizes = lax.axis_size("ty"), lax.axis_size("tx")
    own = [object_tiles[0], object_tiles[1]]
    low0 = shifted(own[0], "ty", -1)
    far = around(object_tiles[1, 1], -1, sizes)
    rgt = [shifted(own[s], "tx", -1) for s in (0, 1)]
    near = shifted(object_tiles[1, 0], "ty", -1)
    (send0,) = call(choose_kernel, [], [own[0], low0], [f32(2, SIDE, SIDE)], flops=10**6)
    low1, send1 = call(join_kernel, [], [near, far, own[1]], [f32(2, SIDE, SIDE)] * 2, flops=10**6)
    low = [low0, low1]
    dia = [moved(send, diagonal_back, sizes) for send in (send0, send1)]

    rolled, prop, ampl = call(
        prepare_kernel, [offsets],
        [probe_field, prop_angle, measured, perm],
        [f32(ITERS, SLOTS, 2, SIDE, SIDE), f32(2, 2, SIDE, HALF), f32(ITERS, SLOTS, 2, SIDE, HALF)],
        [pltpu.VMEM((2, 2 * SIDE, SIDE), jnp.float32)],
    )
    pair, tile = f32(2, 2, SIDE, SIDE), f32(2, SIDE, SIDE)

    tiles = [[own[s], rgt[s], low[s], dia[s]] for s in (0, 1)]

    for iteration in range(ITERS):
        def bind(kernel, iteration=iteration):
            return lambda *refs: kernel(iteration, *refs)

        scalars = [offsets, counts]
        (mid,) = call(bind(first_kernel), scalars, [rolled, prop, tables, *tiles[0]], [pair])
        last = iteration == ITERS - 1
        moves = [pair] if last else [tile, tile]
        stay2, *moves2, carry = call(bind(second_kernel), scalars,
                                     [mid, ampl, tables, *tiles[1]], [pair, *moves, pair])
        stay1, *moves1 = call(bind(third_kernel), scalars,
                              [carry, rolled, prop, tables], [pair, *moves])
        stay = [stay1, stay2]
        if last:
            came = [None, None]
            for s in (1, 0):
                came[s] = shifted([moves1, moves2][s][0], "tx", 1)
            above2, near, far = call(fall_kernel, [], [stay[1], came[1]],
                                     [tile, f32(SIDE, SIDE), f32(SIDE, SIDE)], flops=10**6)
            above1, fallen = call(fall_kernel, [], [stay[0], came[0]], [tile, tile], flops=10**6)
            far = around(far, 1, sizes)
            near = shifted(near, "ty", 1)
            fallen = shifted(fallen, "ty", 1)
            (out,) = call(last_kernel, [], [tiles[0][0], tiles[1][0], above1, above2, near, far, fallen],
                          [pair], flops=10**6)
            return out
        side, diag = [moves1[0], moves2[0]], [moves1[1], moves2[1]]
        for s in (1, 0):
            diag[s] = moved(diag[s], diagonal_on, sizes)
        above, below = [None, None], [None, None]
        for s in (1, 0):
            side[s] = shifted(side[s], "tx", 1)
            above[s], below[s] = call(sums_kernel, [], [stay[s], side[s], diag[s]],
                                      [tile, tile], flops=10**6)
        for s in (1, 0):
            fallen = shifted(below[s], "ty", 1)
            risen = shifted(above[s], "ty", -1)
            own, low, send = call(update_kernel, [],
                                  [above[s], below[s], fallen, risen, tiles[s][0], tiles[s][2]],
                                  [tile] * 3, flops=10**6)
            tiles[s] = [own, shifted(own, "tx", -1), low,
                        moved(send, diagonal_back, sizes)]


def solution(mesh):
    in_specs = (
        P(None, None, "ty", "tx"),
        P(),
        P(),
        P(None, "ty", "tx", None, None),
        P(None, "ty", "tx"),
        P(None, "ty", "tx", None, None, None),
    )
    out_specs = P(None, None, "ty", "tx")

    return jax.shard_map(shards, mesh=mesh, in_specs=in_specs, out_specs=out_specs, check_vma=False)
```

```python
import numpy as np

import jax
import jax.numpy as jnp
from jax import lax
from jax.experimental import pallas as pl
from jax.experimental.pallas import tpu as pltpu
from jax.sharding import PartitionSpec as P


ITERS = 2
SLOTS = 2
SIDE = 256
HALF = SIDE // 2

soft_floor = 0.01
step_size = 0.25


def dft_tables():
    k = np.arange(HALF)
    stack = []
    for parity in (0, 1):
        angle = 2.0 * np.pi * ((2 * k[:, None] + parity) * k[None, :] % SIDE) / SIDE
        cos, sin = np.cos(angle) / 16.0, np.sin(angle) / 16.0
        stack.append(np.block([[cos, sin], [-sin, cos]]))
    both = np.stack([np.stack(stack), np.stack([t.T for t in stack])])
    high = both.astype(jnp.bfloat16)
    low = (both - high.astype(np.float64)).astype(jnp.bfloat16)
    return np.stack([high, low], axis=2)


def shifted(value, axis, steps):
    count = lax.axis_size(axis)
    first, last = (max(0, -steps), min(count, count - steps))
    return lax.ppermute(value, axis, [(source, source + steps) for source in range(first, last)])


def moved(value, target, sizes):
    rows, cols = sizes
    pairs = []
    for row in range(rows):
        for col in range(cols):
            new_row, new_col = target(row, col)
            if 0 <= new_row < rows and 0 <= new_col < cols:
                pairs.append((row * cols + col, new_row * cols + new_col))
    return lax.ppermute(value, ("ty", "tx"), pairs)


NOWHERE = (-1, -1)


def diagonal_back(row, col):
    return (row - 1, col - 1) if col % 4 == 0 else (row, col - 1)


def diagonal_on(row, col):
    return (row + 1, col + 1) if col % 4 == 3 else (row, col + 1)


def around(value, steps, sizes):
    rows, cols = sizes

    def relay(row, col):
        z = (2 * (row % 4) + col // 2 % 2 - 3 * steps) % 8
        return row // 4 * 4 + z // 2, col // 4 * 4 + z % 2 * 2 + col % 2

    spots = [(r, c) for r in range(rows) for c in range(cols) if 0 <= r + steps < rows]
    ends = {relay(*spot): (spot[0] + steps, spot[1]) for spot in spots}
    value = moved(value, lambda r, c: relay(r, c) if (r, c) in spots else NOWHERE, sizes)
    return moved(value, lambda r, c: ends.get((r, c), NOWHERE), sizes)


def split(value):
    high = value.astype(jnp.bfloat16)
    return high, (value - high.astype(jnp.float32)).astype(jnp.bfloat16)


def dot(left, right):
    return jnp.dot(left, right, preferred_element_type=jnp.float32)


def table_left(tables, flip, parity, value):
    high, low = split(value)
    t_high, t_low = tables[flip, parity, 0], tables[flip, parity, 1]
    return dot(t_high, high) + (dot(t_high, low) + dot(t_low, high))


def table_right(tables, flip, parity, value):
    high, low = split(value)
    t_high, t_low = tables[flip, parity, 0], tables[flip, parity, 1]
    return dot(high, t_high) + (dot(low, t_high) + dot(high, t_low))


def rows_cat(a, b):
    return jnp.concatenate([a, b], axis=0)


def lanes_cat(a, b):
    return jnp.concatenate([a, b], axis=1)


def forward(tables, re, im):
    ra, rb, ia, ib = re[:HALF], re[HALF:], im[:HALF], im[HALF:]
    even = table_left(tables, 0, 0, rows_cat(ra + rb, ia + ib))
    odd = table_left(tables, 0, 1, rows_cat(ra - rb, ia - ib))
    real = rows_cat(even[:HALF], odd[:HALF])
    imag = rows_cat(even[HALF:], odd[HALF:])
    ra, rb, ia, ib = real[:, :HALF], real[:, HALF:], imag[:, :HALF], imag[:, HALF:]
    return (
        table_right(tables, 1, 0, lanes_cat(ra + rb, ia + ib)),
        table_right(tables, 1, 1, lanes_cat(ra - rb, ia - ib)),
    )


def inverse(tables, even, odd):
    even = table_right(tables, 0, 0, even)
    odd = table_right(tables, 0, 1, odd)
    real = lanes_cat(even[:, :HALF] + odd[:, :HALF], even[:, :HALF] - odd[:, :HALF])
    imag = lanes_cat(even[:, HALF:] + odd[:, HALF:], even[:, HALF:] - odd[:, HALF:])
    even = table_left(tables, 1, 0, rows_cat(real[:HALF], imag[:HALF]))
    odd = table_left(tables, 1, 1, rows_cat(real[HALF:], imag[HALF:]))
    return (
        rows_cat(even[:HALF] + odd[:HALF], even[:HALF] - odd[:HALF]),
        rows_cat(even[HALF:] + odd[HALF:], even[HALF:] - odd[HALF:]),
    )


def masks(off_ref, iteration, slot):
    row = off_ref[iteration, slot, 0]
    col = off_ref[iteration, slot, 1]
    below = lax.broadcasted_iota(jnp.int32, (SIDE, SIDE), 0) < row
    right = lax.broadcasted_iota(jnp.int32, (SIDE, SIDE), 1) < col
    return below, right


def picked(below, right, own, rgt, low, dia, plane):
    upper = jnp.where(right, rgt[plane], own[plane])
    lower = jnp.where(right, dia[plane], low[plane])
    return jnp.where(below, lower, upper)


def placed(below, right, value, plane, stay, side, diag):
    zero = jnp.zeros_like(value)
    left_part = jnp.where(right, zero, value)
    right_part = jnp.where(right, value, zero)
    stay[0, plane] += jnp.where(below, zero, left_part)
    stay[1, plane] += jnp.where(below, left_part, zero)
    side[plane] += jnp.where(below, zero, right_part)
    diag[plane] += jnp.where(below, right_part, zero)


def prepare_kernel(off_ref, probe_ref, angle_ref, amp_ref, perm_ref,
                   rolled_ref, prop_ref, ampl_ref, twice):
    def reorder(src):
        rest = src
        total = None
        for _ in range(3):
            part = rest.astype(jnp.bfloat16)
            rest = rest - part.astype(jnp.float32)
            part = dot(dot(perm_ref[0], part).astype(jnp.bfloat16), perm_ref[1])
            total = part if total is None else total + part
        return total

    def put(dst, value):
        dst[0] = value[:, :HALF]
        dst[1] = value[:, HALF:]

    def tile_loop(index, carry):
        it, slot = index // SLOTS, index % SLOTS
        row = off_ref[it, slot, 0]
        col = off_ref[it, slot, 1]
        for plane in range(2):
            start = pl.multiple_of(SIDE - 8 - row // 8 * 8, 8)
            turned = pltpu.roll(twice[plane, pl.ds(start, SIDE + 8), :], row % 8, 0)
            rolled_ref[it, slot, plane] = pltpu.roll(turned[8:], col, 1)
        put(ampl_ref.at[it, slot], reorder(amp_ref[it, slot]))
        return carry

    for plane in range(2):
        twice[plane, :SIDE] = probe_ref[plane]
        twice[plane, SIDE:] = probe_ref[plane]
    put(prop_ref.at[0], reorder(jnp.cos(angle_ref[...])))
    put(prop_ref.at[1], reorder(jnp.sin(angle_ref[...])))
    lax.fori_loop(0, ITERS * SLOTS, tile_loop, 0)


def first_kernel(iteration, off_ref, cnt_ref, rolled, prop, tables, *refs):
    *tiles, mid_ref = refs
    own, rgt, low, dia = tiles

    def body(slot, carry):
        below, right = masks(off_ref, iteration, slot)
        one_re = picked(below, right, own, rgt, low, dia, 0)
        one_im = picked(below, right, own, rgt, low, dia, 1)
        p_re, p_im = rolled[iteration, slot, 0], rolled[iteration, slot, 1]
        spec = forward(tables, p_re * one_re - p_im * one_im, p_re * one_im + p_im * one_re)
        moved = []
        for q in range(2):
            re, im = spec[q][:, :HALF], spec[q][:, HALF:]
            h_re, h_im = prop[0, q], prop[1, q]
            moved.append(lanes_cat(re * h_re - im * h_im, re * h_im + im * h_re))
        mid_ref[slot, 0], mid_ref[slot, 1] = inverse(tables, *moved)
        return carry

    lax.fori_loop(0, cnt_ref[iteration], body, 0)


def second_kernel(iteration, off_ref, cnt_ref, mid_ref, ampl, tables, *refs):
    own, rgt, low, dia, stay, *moves, carry_ref = refs
    side, diag = moves if len(moves) == 2 else (moves[0].at[0], moves[0].at[1])
    stay[...] = jnp.zeros_like(stay)
    side[...] = jnp.zeros_like(side)
    diag[...] = jnp.zeros_like(diag)

    def body(slot, carry):
        below, right = masks(off_ref, iteration, slot)
        two_re = picked(below, right, own, rgt, low, dia, 0)
        two_im = picked(below, right, own, rgt, low, dia, 1)
        m_re, m_im = mid_ref[slot, 0], mid_ref[slot, 1]
        far = forward(tables, m_re * two_re - m_im * two_im, m_re * two_im + m_im * two_re)
        chi = []
        for q in range(2):
            re, im = far[q][:, :HALF], far[q][:, HALF:]
            factor = 1.0 - ampl[iteration, slot, q] * lax.rsqrt(re * re + im * im + soft_floor)
            chi.append(lanes_cat(re * factor, im * factor))
        b_re, b_im = inverse(tables, *chi)
        placed(below, right, m_re * b_re + m_im * b_im, 0, stay, side, diag)
        placed(below, right, m_re * b_im - m_im * b_re, 1, stay, side, diag)
        carry_ref[slot, 0] = two_re * b_re + two_im * b_im
        carry_ref[slot, 1] = two_re * b_im - two_im * b_re
        return carry

    lax.fori_loop(0, cnt_ref[iteration], body, 0)


def third_kernel(iteration, off_ref, cnt_ref, carry_ref, rolled, prop, tables, stay, *moves):
    side, diag = moves if len(moves) == 2 else (moves[0].at[0], moves[0].at[1])
    stay[...] = jnp.zeros_like(stay)
    side[...] = jnp.zeros_like(side)
    diag[...] = jnp.zeros_like(diag)

    def body(slot, carry):
        below, right = masks(off_ref, iteration, slot)
        spec = forward(tables, carry_ref[slot, 0], carry_ref[slot, 1])
        turned = []
        for q in range(2):
            re, im = spec[q][:, :HALF], spec[q][:, HALF:]
            h_re, h_im = prop[0, q], prop[1, q]
            turned.append(lanes_cat(re * h_re + im * h_im, im * h_re - re * h_im))
        e_re, e_im = inverse(tables, *turned)
        p_re, p_im = rolled[iteration, slot, 0], rolled[iteration, slot, 1]
        placed(below, right, p_re * e_re + p_im * e_im, 0, stay, side, diag)
        placed(below, right, p_re * e_im - p_im * e_re, 1, stay, side, diag)
        return carry

    lax.fori_loop(0, cnt_ref[iteration], body, 0)


def leading():
    return lax.rem(lax.axis_index("tx"), 4) == 0


def join_kernel(near, far, own, both, send):
    for plane, part in enumerate((near, far)):
        both[plane] = part[...]
        send[plane] = jnp.where(leading(), own[plane], part[...])


def choose_kernel(own, low, send):
    for plane in range(2):
        send[plane] = jnp.where(leading(), own[plane], low[plane])


def sums_kernel(stay, side, diag, above, below):
    for plane in range(2):
        zero = jnp.zeros((SIDE, SIDE), jnp.float32)
        extra = diag[plane]
        above[plane] = stay[0, plane] + side[plane] + jnp.where(leading(), extra, zero)
        below[plane] = stay[1, plane] + jnp.where(leading(), zero, extra)


def fall_kernel(stay, diag, *below):
    for plane in range(2):
        total = stay[1, plane] + jnp.where(leading(), jnp.zeros((SIDE, SIDE), jnp.float32), diag[plane])
        if len(below) == 1:
            below[0][plane] = total
        else:
            below[plane][...] = total


def update_kernel(above, below, from_above, from_below, old, old_low, own, low, send):
    for plane in range(2):
        one = old[plane] - step_size * (above[plane] + from_above[plane])
        two = old_low[plane] - step_size * (from_below[plane] + below[plane])
        own[plane] = one
        low[plane] = two
        send[plane] = jnp.where(leading(), one, two)


def last_kernel(one, two, stay1, side1, diag1, stay2, side2, diag2, near2, far2, fallen1, out):
    for s, (old, stay, side, diag) in enumerate(((one, stay1, side1, diag1), (two, stay2, side2, diag2))):
        for plane in range(2):
            extra = jnp.where(leading(), diag[plane], jnp.zeros((SIDE, SIDE), jnp.float32))
            fallen = fallen1[plane] if s == 0 else (near2, far2)[plane][...]
            out[s, plane] = old[plane] - step_size * (stay[0, plane] + side[plane] + extra + fallen)


SMEM = pl.BlockSpec(memory_space=pltpu.SMEM)
VMEM = pl.BlockSpec(memory_space=pltpu.VMEM)
LIMIT = 12 * 1024 * 1024


def f32(*shape):
    return jax.ShapeDtypeStruct(shape, jnp.float32)


def call(body, scalars, arrays, outs, scratch=(), flops=4 * 10**9):
    args = [*scalars, *arrays]
    return pl.pallas_call(
        body,
        out_shape=outs,
        in_specs=[SMEM] * len(scalars) + [VMEM] * len(arrays),
        out_specs=[VMEM] * len(outs),
        scratch_shapes=scratch,
        compiler_params=pltpu.CompilerParams(vmem_limit_bytes=LIMIT),
        cost_estimate=pl.CostEstimate(flops=flops, bytes_accessed=8 * 2**20, transcendentals=0),
    )(*args)


def shards(object_tiles, probe_field, prop_angle, scan_offsets, probe_counts, amplitudes):
    tables = jnp.asarray(dft_tables())
    lane = np.arange(SIDE)
    source = np.concatenate([lane[0::2], lane[1::2]])
    perm = np.zeros((SIDE, SIDE), np.float32)
    perm[source, lane] = 1.0
    perm = jnp.asarray(np.stack([perm.T, perm]).astype(jnp.bfloat16))
    offsets = scan_offsets.reshape(ITERS, SLOTS, 2)
    counts = probe_counts.reshape(ITERS)
    measured = amplitudes.reshape(ITERS, SLOTS, SIDE, SIDE)

    sizes = lax.axis_size("ty"), lax.axis_size("tx")
    sizes = lax.axis_size("ty"), lax.axis_size("tx")
    own = [object_tiles[0], object_tiles[1]]
    low0 = shifted(own[0], "ty", -1)
    far = around(object_tiles[1, 1], -1, sizes)
    rgt = [shifted(own[s], "tx", -1) for s in (0, 1)]
    near = shifted(object_tiles[1, 0], "ty", -1)
    (send0,) = call(choose_kernel, [], [own[0], low0], [f32(2, SIDE, SIDE)], flops=10**6)
    low1, send1 = call(join_kernel, [], [near, far, own[1]], [f32(2, SIDE, SIDE)] * 2, flops=10**6)
    low = [low0, low1]
    dia = [moved(send, diagonal_back, sizes) for send in (send0, send1)]

    rolled, prop, ampl = call(
        prepare_kernel, [offsets],
        [probe_field, prop_angle, measured, perm],
        [f32(ITERS, SLOTS, 2, SIDE, SIDE), f32(2, 2, SIDE, HALF), f32(ITERS, SLOTS, 2, SIDE, HALF)],
        [pltpu.VMEM((2, 2 * SIDE, SIDE), jnp.float32)],
    )
    pair, tile = f32(2, 2, SIDE, SIDE), f32(2, SIDE, SIDE)

    tiles = [[own[s], rgt[s], low[s], dia[s]] for s in (0, 1)]

    for iteration in range(ITERS):
        def bind(kernel, iteration=iteration):
            return lambda *refs: kernel(iteration, *refs)

        scalars = [offsets, counts]
        (mid,) = call(bind(first_kernel), scalars, [rolled, prop, tables, *tiles[0]], [pair])
        last = iteration == ITERS - 1
        moves = [tile, tile]
        stay2, *moves2, carry = call(bind(second_kernel), scalars,
                                     [mid, ampl, tables, *tiles[1]], [pair, *moves, pair])
        stay1, *moves1 = call(bind(third_kernel), scalars,
                              [carry, rolled, prop, tables], [pair, *moves])
        stay = [stay1, stay2]
        side, diag = [moves1[0], moves2[0]], [moves1[1], moves2[1]]
        for s in (1, 0):
            diag[s] = moved(diag[s], diagonal_on, sizes)
        if last:
            near, far = call(fall_kernel, [], [stay[1], diag[1]], [f32(SIDE, SIDE)] * 2, flops=10**6)
            (fallen,) = call(fall_kernel, [], [stay[0], diag[0]], [tile], flops=10**6)
            far = around(far, 1, sizes)
            near = shifted(near, "ty", 1)
            fallen = shifted(fallen, "ty", 1)
            side = [shifted(side[s], "tx", 1) for s in (0, 1)]
            (out,) = call(last_kernel, [],
                          [tiles[0][0], tiles[1][0], stay[0], side[0], diag[0], stay[1], side[1], diag[1],
                           near, far, fallen], [pair], flops=10**6)
            return out
        above, below = [None, None], [None, None]
        for s in (1, 0):
            side[s] = shifted(side[s], "tx", 1)
            above[s], below[s] = call(sums_kernel, [], [stay[s], side[s], diag[s]],
                                      [tile, tile], flops=10**6)
        for s in (1, 0):
            fallen = shifted(below[s], "ty", 1)
            risen = shifted(above[s], "ty", -1)
            own, low, send = call(update_kernel, [],
                                  [above[s], below[s], fallen, risen, tiles[s][0], tiles[s][2]],
                                  [tile] * 3, flops=10**6)
            tiles[s] = [own, shifted(own, "tx", -1), low,
                        moved(send, diagonal_back, sizes)]


def solution(mesh):
    in_specs = (
        P(None, None, "ty", "tx"),
        P(),
        P(),
        P(None, "ty", "tx", None, None),
        P(None, "ty", "tx"),
        P(None, "ty", "tx", None, None, None),
    )
    out_specs = P(None, None, "ty", "tx")

    return jax.shard_map(shards, mesh=mesh, in_specs=in_specs, out_specs=out_specs, check_vma=False)
```
